32 devices in a mesh: dp: 1, mp: 32 (over z, y, x, core).
Axes of the slice: x: 2, y: 2, z: 4, core: 2. Of those that a mesh axis runs over, the one named last changes fastest.
Arguments:
- activations: bfloat16 [2048, 8192], P('dp', 'mp'), may hold values from -6 to 6
- w_up: bfloat16 [5, 256, 32768], P(None, None, 'mp'), may hold values from -0.15625 to 0.15625
- w_down: bfloat16 [5, 32768, 256], P(None, 'mp'), may hold values from -0.078125 to 0.078125
- u_up: bfloat16 [8192, 128], P('mp'), may hold values from -0.0625 to 0.0625
- v_up: bfloat16 [128, 32768], P(None, 'mp'), may hold values from -0.5 to 0.5
- u_down: bfloat16 [32768, 128], P('mp'), may hold values from -0.03125 to 0.03125
- v_down: bfloat16 [128, 8192], P(None, 'mp'), may hold values from -0.5 to 0.5
- mask_up: int32 [4, 32], P(None, 'mp'), may hold values 0 or 1
- mask_down: int32 [4, 32], P(None, 'mp'), may hold values 0 or 1
- grad_y: bfloat16 [2048, 8192], P('dp', 'mp'), may hold values from -6 to 6
Outputs:
- output: bfloat16 [2048, 8192], P('dp', 'mp')
- grad_x: bfloat16 [2048, 8192], P('dp', 'mp')
- grad_w_up: float32 [5, 256, 32768], P(None, None, 'mp')
- grad_w_down: float32 [5, 32768, 256], P(None, 'mp')
- grad_u_up: float32 [8192, 128], P('mp')
- grad_v_up: float32 [128, 32768], P(None, 'mp')
- grad_u_down: float32 [32768, 128], P('mp')
- grad_v_down: float32 [128, 8192], P(None, 'mp')
The draws below stay inside these ranges and needn't reach their ends.
All inputs are finite; a program needn't handle non-finite values. No bound on the sum of `mask_up` or of `mask_down` on one device may be relied on, other than what follows from the above.
Results may differ from the reference program's by a relative error of at most 0.008.
Values may be sent and summed in bfloat16 or wider, within the bound.
A program may use at most 192 MiB of HBM per device.

```python
import jax
import jax.numpy as jnp

D = 8192
FF = 32768
RANK = 128
LEVELS = 4
TOKENS = 2048
DG = 256
HG = 1024
N_MP = 32


def touch_ends(drawn, stream_key, low, largest):
    index_at = [jax.random.randint(jax.random.fold_in(stream_key, axis), (), 0, length) for axis, length in enumerate(drawn.shape)]
    main_axis = drawn.shape.index(max(drawn.shape))
    next_to = index_at[:main_axis] + [(index_at[main_axis] + 1) % drawn.shape[main_axis]] + index_at[main_axis + 1:]
    return drawn.at[tuple(index_at)].set(low).at[tuple(next_to)].set(largest)


def level_of(stream_key, dims, pieces, low, top_value):
    def one(axis_at, shards_of):
        heights = jax.random.uniform(jax.random.fold_in(jax.random.fold_in(stream_key, 6), axis_at), (shards_of,), jnp.float32, low / len(pieces), top_value / len(pieces))
        return jnp.repeat(jnp.exp(heights), dims[axis_at] // shards_of).reshape((-1,) + (1,) * (len(dims) - axis_at - 1))

    gain = one(*pieces[0])
    for cut in pieces[1:]:
        gain = gain * one(*cut)
    return gain


def gaussian(rng, shape, deviation, limit, shards=(), held_as=jnp.bfloat16):
    drawn = jax.random.normal(rng, shape, jnp.float32) * deviation
    if len(shards) > 0:
        drawn = level_of(rng, shape, shards, -0.22, 0.18) * drawn
    return jnp.clip(drawn, min=-limit, max=limit).astype(held_as)


def setup_inputs(seed: int = 0) -> dict:
    splits = jax.random.split(jax.random.key(seed), 11)
    activations = gaussian(splits[0], (TOKENS, D), 1.0, 6.0, ((1, 32),))
    w_up = gaussian(splits[1], (LEVELS + 1, DG, FF), ((LEVELS + 1) * DG) ** -0.5, 0.15625, ((2, 32),))
    w_down = gaussian(splits[2], (LEVELS + 1, FF, DG), ((LEVELS + 1) * HG) ** -0.5, 0.078125, ((1, 32),))
    u_up = gaussian(splits[3], (D, RANK), D ** -0.5, 0.0625, ((0, 32),))
    v_up = gaussian(splits[4], (RANK, FF), RANK ** -0.5, 0.5, ((1, 32),))
    u_down = gaussian(splits[5], (FF, RANK), FF ** -0.5, 0.03125, ((0, 32),))
    v_down = gaussian(splits[6], (RANK, D), RANK ** -0.5, 0.5, ((1, 32),))
    mask_up = touch_ends((jax.random.randint(splits[7], (LEVELS, N_MP), 0, 4) < 3).astype(jnp.int32), jax.random.fold_in(splits[7], 1), 0, 1)
    mask_down = touch_ends((jax.random.randint(splits[8], (LEVELS, N_MP), 0, 4) < 3).astype(jnp.int32), jax.random.fold_in(splits[8], 1), 0, 1)
    grad_y = gaussian(splits[9], (TOKENS, D), 1.0, 6.0, ((1, 32),))
    return {"activations": activations, "w_up": w_up, "w_down": w_down, "u_up": u_up, "v_up": v_up, "u_down": u_down, "v_down": v_down, "mask_up": mask_up, "mask_down": mask_down, "grad_y": grad_y}


def gelu_tanh(value):
    return jax.nn.gelu(value, approximate=True)

def reference(activations, w_up, w_down, u_up, v_up, u_down, v_down, mask_up, mask_down, grad_y):
    f32 = jnp.float32
    groups = jnp.arange(N_MP, dtype=jnp.int32)
    x_blocks = activations.astype(f32).reshape(TOKENS, N_MP, DG)
    wu_blocks = w_up.astype(f32).reshape(LEVELS + 1, DG, N_MP, HG)
    wd_blocks = w_down.astype(f32).reshape(LEVELS + 1, N_MP, HG, DG)
    mu_float = mask_up.astype(f32)
    md_float = mask_down.astype(f32)
    z_up = jnp.dot(activations, u_up, preferred_element_type=f32).astype(jnp.bfloat16)
    pre = jnp.einsum('tgd,dgh->tgh', x_blocks, wu_blocks[0])
    for level in range(LEVELS):
        partner = jnp.bitwise_xor(groups, jnp.int32(1 << level))
        term = jnp.einsum('tgd,dgh->tgh', x_blocks[:, partner], wu_blocks[level + 1])
        pre = pre + term * mu_float[level][None, :, None]
    pre = pre.reshape(TOKENS, FF) + jnp.dot(z_up, v_up, preferred_element_type=f32)
    hidden = gelu_tanh(pre).astype(jnp.bfloat16)
    hid_blocks = hidden.astype(f32).reshape(TOKENS, N_MP, HG)
    z_down = jnp.dot(hidden, u_down, preferred_element_type=f32).astype(jnp.bfloat16)
    out = jnp.einsum('tgh,ghd->tgd', hid_blocks, wd_blocks[0])
    for level in range(LEVELS):
        partner = jnp.bitwise_xor(groups, jnp.int32(1 << level))
        term = jnp.einsum('tgh,ghd->tgd', hid_blocks[:, partner], wd_blocks[level + 1][partner])
        out = out + term * md_float[level][None, :, None]
    output = (out.reshape(TOKENS, D) + jnp.dot(z_down, v_down, preferred_element_type=f32)).astype(jnp.bfloat16)
    gy_blocks = grad_y.astype(f32).reshape(TOKENS, N_MP, DG)
    grad_v_down = jnp.dot(z_down.T, grad_y, preferred_element_type=f32)
    gz_down = jnp.dot(grad_y, v_down.T, preferred_element_type=f32).astype(jnp.bfloat16)
    grad_u_down = jnp.dot(hidden.T, gz_down, preferred_element_type=f32)
    gwd_list = [jnp.einsum('tgh,tgd->ghd', hid_blocks, gy_blocks)]
    grad_hid = jnp.einsum('tgd,ghd->tgh', gy_blocks, wd_blocks[0])
    for level in range(LEVELS):
        partner = jnp.bitwise_xor(groups, jnp.int32(1 << level))
        masked = gy_blocks[:, partner] * md_float[level][partner][None, :, None]
        gwd_list.append(jnp.einsum('tgh,tgd->ghd', hid_blocks, masked))
        grad_hid = grad_hid + jnp.einsum('tgd,ghd->tgh', masked, wd_blocks[level + 1])
    grad_w_down = jnp.stack(gwd_list).reshape(LEVELS + 1, FF, DG)
    grad_hid = grad_hid.reshape(TOKENS, FF) + jnp.dot(gz_down, u_down.T, preferred_element_type=f32)
    unused, pullback = jax.vjp(gelu_tanh, pre)
    grad_pre = pullback(grad_hid)[0].astype(jnp.bfloat16)
    grad_v_up = jnp.dot(z_up.T, grad_pre, preferred_element_type=f32)
    gz_up = jnp.dot(grad_pre, v_up.T, preferred_element_type=f32).astype(jnp.bfloat16)
    grad_u_up = jnp.dot(activations.T, gz_up, preferred_element_type=f32)
    gp_blocks = grad_pre.astype(f32).reshape(TOKENS, N_MP, HG)
    gwu_list = [jnp.einsum('tgd,tgh->dgh', x_blocks, gp_blocks)]
    grad_in = jnp.einsum('tgh,dgh->tgd', gp_blocks, wu_blocks[0])
    for level in range(LEVELS):
        partner = jnp.bitwise_xor(groups, jnp.int32(1 << level))
        gwu_list.append(jnp.einsum('tgd,tgh->dgh', x_blocks[:, partner], gp_blocks) * mu_float[level][None, :, None])
        masked = gp_blocks * mu_float[level][None, :, None]
        term = jnp.einsum('tgh,dgh->tgd', masked, wu_blocks[level + 1])
        grad_in = grad_in + term[:, partner]
    grad_w_up = jnp.stack(gwu_list).reshape(LEVELS + 1, DG, FF)
    grad_x = (grad_in.reshape(TOKENS, D) + jnp.dot(gz_up, u_up.T, preferred_element_type=f32)).astype(jnp.bfloat16)
    return (output, grad_x, grad_w_up, grad_w_down, grad_u_up, grad_v_up, grad_u_down, grad_v_down)
```

```python
import functools

import jax
import jax.numpy as jnp
from jax import lax
from jax.experimental import pallas as pl
from jax.experimental.pallas import tpu as pltpu
from jax.sharding import PartitionSpec as P

CHUNKS = 4
PIECES = 4
ROWS = 256
COLUMNS = 256
ROOT = 0.7978845608028654
CUBIC = 0.044715
VMEM_LIMIT = 67043328
MESH = pl.DeviceIdType.MESH
EARLY_ISSUE = ((2, 2, 2), (0, 2, 2), (2, 0, 1), (0, 1, 0), (1, 1, 0), (1, 1, 0), (1, 1, 1), (1, 0, 2), (0, 2, 2), (2, 2, 2))
CHUNK_ISSUE = 2
LATE_ISSUE = ((0, 0, 0), (1, 1, 0), (1, 0, 1), (0, 1, 1), (1, 1, 0), (1, 1, 0), (0, 1, 1), (1, 0, 1), (2, 2, 0), (1, 1, 2))


def dot(left, right):
    return jnp.dot(left, right, preferred_element_type=jnp.float32)


def dot_nt(left, right):
    return lax.dot_general(left, right, (((1,), (1,)), ((), ())), preferred_element_type=jnp.float32)


def dot_tn(left, right):
    return lax.dot_general(left, right, (((0,), (0,)), ((), ())), preferred_element_type=jnp.float32)


class Sum:
    def __init__(self, me, order, acc, sent, got, held, send_sems, recv_sems):
        self.me, self.order = me, order
        self.acc, self.sent, self.got, self.held = acc, sent, got, held
        self.send_sems, self.recv_sems = send_sems, recv_sems
        self.base, self.length, self.offset = jnp.int32(0), acc.shape[0], 0
        self.rounds = len(order)
        self.copy = None

    def bit(self, level):
        return lax.rem(lax.div(self.me, jnp.int32(1 << level)), jnp.int32(2))

    def rows(self, base, length):
        return pl.ds(pl.multiple_of(base, length), length)

    def remote(self, src, dst, step, level):
        self.copy = pltpu.make_async_remote_copy(
            src_ref=src, dst_ref=dst, send_sem=self.send_sems.at[step], recv_sem=self.recv_sems.at[step],
            device_id={"mp": partner(self.me, level)}, device_id_type=MESH,
        )
        self.copy.start()

    def start(self, step):
        if step < self.rounds:
            level = self.order[step]
            half = self.length // 2
            bit = self.bit(level)
            here = pl.ds(self.offset, half)
            self.sent[here, :] = self.acc[self.rows(self.base + (1 - bit) * half, half), :].astype(jnp.bfloat16)
            self.remote(self.sent.at[here], self.got.at[here], step, level)
        else:
            level = self.order[2 * self.rounds - 1 - step]
            if step == self.rounds:
                mine = self.rows(self.base, self.length)
                self.held[mine, :] = self.acc[mine, :].astype(jnp.bfloat16)
            mine = self.held.at[self.rows(self.base, self.length)]
            self.remote(mine, mine, step, level)

    def finish(self, step):
        self.copy.wait()
        if step < self.rounds:
            half = self.length // 2
            self.base = self.base + self.bit(self.order[step]) * half
            kept = self.rows(self.base, half)
            self.acc[kept, :] = self.acc[kept, :] + self.got[pl.ds(self.offset, half), :].astype(jnp.float32)
            self.offset += half
            self.length = half
        else:
            level = self.order[2 * self.rounds - 1 - step]
            self.base = self.base - self.bit(level) * self.length
            self.length *= 2


def partner(me, level):
    step = 1 << level
    bit = lax.rem(lax.div(me, jnp.int32(step)), jnp.int32(2))
    return me + (1 - 2 * bit) * step


def kernel(rounds, mu_ref, md_ref, x_hbm, gy_hbm, wu_hbm, wd_hbm, uu_hbm, vu_hbm, ud_hbm, vd_hbm,
           out_hbm, gx_hbm, gwu_hbm, gwd_hbm, guu_hbm, gvu_hbm, gud_hbm, gvd_hbm,
           xs, wu, wd, uu, vu, ud, vd, hid, gp, put, came, diag, acc, zs, zl, sent_e, got_e, sent_l, got_l,
           stage_up, stage_down, out_v, gx_v, guu, gvu, gud, gvd, mask_mine, mask_theirs,
           load_sems, mask_send, mask_recv, in_send, in_recv, put_send, put_recv, es, er, ls, lr, store_sems):
    slabs, tokens = xs.shape[:2]
    levels = slabs - 1
    width, hidden = wu.shape[1:]
    rank = vu.shape[0]
    chunk = tokens // CHUNKS
    piece = chunk // PIECES
    pieces = CHUNKS * PIECES
    step = min(COLUMNS, hidden)
    me = lax.axis_index("mp")

    loads = []
    for i, (src, dst) in enumerate((
        (x_hbm, xs.at[0, :, pl.ds(0, width)]), (gy_hbm, xs.at[0, :, pl.ds(width, width)]),
        (uu_hbm, uu), (vd_hbm, vd), (wu_hbm, wu), (wd_hbm, wd), (vu_hbm, vu), (ud_hbm, ud),
    )):
        loads.append(pltpu.make_async_copy(src, dst, load_sems.at[i]))
        loads[-1].start()

    barrier = pltpu.get_barrier_semaphore()
    for level in range(rounds):
        pl.semaphore_signal(barrier, inc=1, device_id={"mp": partner(me, level)}, device_id_type=MESH)
    for k in range(levels):
        mask_mine[8 * k:8 * k + 8, :] = jnp.full((8, 128), md_ref[k].astype(jnp.float32))
    pl.semaphore_wait(barrier, rounds)

    def mask_copy(k):
        here = pl.ds(8 * k, 8)
        return pltpu.make_async_remote_copy(
            src_ref=mask_mine.at[here], dst_ref=mask_theirs.at[here], send_sem=mask_send.at[k], recv_sem=mask_recv.at[k],
            device_id={"mp": partner(me, k)}, device_id_type=MESH)

    def input_copy(k, start, length):
        rows = pl.ds(start, length)
        return pltpu.make_async_remote_copy(
            src_ref=xs.at[0, rows], dst_ref=xs.at[k + 1, rows], send_sem=in_send.at[k], recv_sem=in_recv.at[k, lax.div(start, chunk)],
            device_id={"mp": partner(me, k)}, device_id_type=MESH)

    def partial_copy(k, start, length):
        rows = pl.ds(start, length)
        return pltpu.make_async_remote_copy(
            src_ref=put.at[k, rows], dst_ref=came.at[k, rows], send_sem=put_send.at[k], recv_sem=put_recv.at[k, lax.div(start, chunk)],
            device_id={"mp": partner(me, k)}, device_id_type=MESH)

    in_done = [0] * levels
    put_done = [0] * levels

    def issue(copy, done, k, count):
        for i in range(done[k], min(pieces, done[k] + count)):
            copy(k, i * piece, piece).start()
        done[k] = min(pieces, done[k] + count)

    loads[0].wait()
    loads[1].wait()
    for k in range(levels):
        mask_copy(k).start()
    issue(input_copy, in_done, 0, PIECES)
    for k in range(1, levels):
        issue(input_copy, in_done, k, EARLY_ISSUE[0][k - 1])
    loads[2].wait()
    loads[3].wait()

    @pl.loop(0, CHUNKS)
    def _(c):
        rows = pl.ds(pl.multiple_of(c * chunk, chunk), chunk)
        acc[rows, :rank] = dot(xs[0, rows, :width], uu[...])
        acc[rows, rank:] = dot_nt(xs[0, rows, width:], vd[...])

    early = Sum(me, tuple(range(rounds)), acc, sent_e, got_e, zs, es, er)
    for s in range(2 * rounds):
        early.start(s)
        if s == 0:
            issue(input_copy, in_done, 0, pieces)
        elif s < len(EARLY_ISSUE):
            for k in range(1, levels):
                issue(input_copy, in_done, k, EARLY_ISSUE[s][k - 1])
        if s == 0:
            loads[4].wait()
            for k in range(levels):
                wu[k + 1] = (wu[k + 1].astype(jnp.float32) * mu_ref[k].astype(jnp.float32)).astype(jnp.bfloat16)
        if s == 1:
            loads[5].wait()
            for k in range(levels):
                mask_copy(k).wait()
                row = jnp.concatenate([mask_theirs[8 * k:8 * k + 1, :]] * (width // 128), axis=1)
                wd[k + 1] = (wd[k + 1].astype(jnp.float32) * row).astype(jnp.bfloat16)
        if s == 2:
            loads[6].wait()
            loads[7].wait()
        early.finish(s)
    for k in range(1, levels):
        issue(input_copy, in_done, k, pieces)

    @pl.loop(0, CHUNKS)
    def _(c):
        for k in range(levels):
            input_copy(k, c * chunk, chunk).wait_recv()

        @pl.loop(0, chunk // ROWS)
        def _(r):
            rows = pl.ds(pl.multiple_of(c * chunk + r * ROWS, ROWS), ROWS)
            for start in range(0, hidden, step):
                cols = slice(start, start + step)
                v = dot(zs[rows, :rank], vu[:, cols])
                gh = dot_nt(zs[rows, rank:], ud[cols, :])
                for k in range(slabs):
                    v += dot(xs[k, rows, :width], wu[k, :, cols])
                    gh += dot_nt(xs[k, rows, width:], wd[k, cols, :])
                square = v * v
                half_tanh = 0.5 * jnp.tanh(v * (ROOT + (ROOT * CUBIC) * square))
                gate = 0.5 + half_tanh
                hid[rows, cols] = (v * gate).astype(jnp.bfloat16)
                slope = gate + v * (0.5 - 2.0 * half_tanh * half_tanh) * (ROOT + (3.0 * ROOT * CUBIC) * square)
                gp[rows, cols] = (gh * slope).astype(jnp.bfloat16)
            h = hid[rows, :]
            g = gp[rows, :]
            for k in range(levels):
                put[k, rows, :width] = dot(h, wd[k + 1]).astype(jnp.bfloat16)
                put[k, rows, width:] = dot_nt(g, wu[k + 1]).astype(jnp.bfloat16)
            acc[rows, :rank] = dot(h, ud[...])
            acc[rows, rank:] = dot_nt(g, vu[...])
            diag[rows, :width] = dot(h, wd[0])
            diag[rows, width:] = dot_nt(g, wu[0])

        partial_copy(0, c * chunk, chunk).start()
        for k in range(1, levels):
            for i in range(CHUNK_ISSUE):
                partial_copy(k, (c * CHUNK_ISSUE + i) * piece, piece).start()

    for k in range(levels):
        put_done[k] = pieces if k == 0 else CHUNKS * CHUNK_ISSUE

    stores = []

    def store(src, dst):
        stores.append(pltpu.make_async_copy(src, dst, store_sems.at[len(stores)]))
        stores[-1].start()
        return stores[-1]

    held = [None, None]
    pending = []

    def slab_grads(k):
        slot = k % 2
        if held[slot]:
            for copy in held[slot]:
                copy.wait()
                pending.remove(copy)
        for start in range(0, width, ROWS):
            stop = min(width, start + ROWS)
            up = dot_tn(xs[k, :, start:stop], gp[...])
            if k:
                up = up * mu_ref[k - 1].astype(jnp.float32)
            stage_up[slot, start:stop, :] = up

        @pl.loop(0, hidden // step)
        def _(b):
            cols = pl.ds(pl.multiple_of(b * step, step), step)
            down = dot_tn(hid[:, cols], xs[k, :, width:])
            if k:
                down = down * jnp.concatenate([mask_theirs[8 * k - 8:8 * k - 7, :]] * (width // 128), axis=1)
            stage_down[slot, cols, :] = down

        held[slot] = (store(stage_up.at[slot], gwu_hbm.at[k]), store(stage_down.at[slot], gwd_hbm.at[k]))
        pending.extend(held[slot])

    late = Sum(me, (0,) + tuple(range(levels - 1, 0, -1)) + tuple(range(levels, rounds)), acc, sent_l, got_l, zl, ls, lr)
    for s in range(2 * rounds):
        late.start(s)
        if s < len(LATE_ISSUE):
            for k in range(1, levels):
                issue(partial_copy, put_done, k, LATE_ISSUE[s][k - 1])
        if 1 <= s <= slabs:
            slab_grads(s - 1)
        if s == slabs + 1:
            gvu[...] = dot_tn(zs[:, :rank], gp[...])
            pending.append(store(gvu, gvu_hbm))
            gud[...] = dot_tn(hid[...], zs[:, rank:])
            pending.append(store(gud, gud_hbm))
        late.finish(s)
    for k in range(1, levels):
        issue(partial_copy, put_done, k, pieces)

    guu[...] = dot_tn(xs[0, :, :width], zl[:, rank:])
    pending.append(store(guu, guu_hbm))
    gvd[...] = dot_tn(zl[:, :rank], xs[0, :, width:])
    pending.append(store(gvd, gvd_hbm))

    for c in range(CHUNKS):
        rows = pl.ds(c * chunk, chunk)
        out = diag[rows, :width] + dot(zl[rows, :rank], vd[...])
        gx = diag[rows, width:] + dot_nt(zl[rows, rank:], uu[...])
        for k in range(levels):
            partial_copy(k, c * chunk, chunk).wait_recv()
            out = out + came[k, rows, :width].astype(jnp.float32)
            gx = gx + came[k, rows, width:].astype(jnp.float32)
        out_v[rows, :] = out.astype(jnp.bfloat16)
        gx_v[rows, :] = gx.astype(jnp.bfloat16)
        pending.append(store(out_v.at[rows], out_hbm.at[rows]))
        pending.append(store(gx_v.at[rows], gx_hbm.at[rows]))
    for copy in pending:
        copy.wait()
    for k in range(levels):
        input_copy(k, 0, tokens).wait_send()
        partial_copy(k, 0, tokens).wait_send()


def summed_over_dp(array):
    if lax.axis_size("dp") == 1:
        return array
    return lax.psum(array.astype(jnp.bfloat16), "dp").astype(jnp.float32)


def per_device(activations, w_up, w_down, u_up, v_up, u_down, v_down, mask_up, mask_down, grad_y):
    bf, f32 = jnp.bfloat16, jnp.float32
    slabs, width, hidden = w_up.shape
    tokens = activations.shape[0]
    rank = v_up.shape[0]
    levels = slabs - 1
    rounds = lax.axis_size("mp").bit_length() - 1
    vmem = pltpu.VMEM
    dma = lambda *shape: pltpu.SemaphoreType.DMA(shape)
    shape = jax.ShapeDtypeStruct
    outs = [
        shape((tokens, width), bf), shape((tokens, width), bf), shape((slabs, width, hidden), f32), shape((slabs, hidden, width), f32),
        shape((width, rank), f32), shape((rank, hidden), f32), shape((hidden, rank), f32), shape((rank, width), f32),
    ]
    scratch = [
        vmem((slabs, tokens, 2 * width), bf), vmem(w_up.shape, bf), vmem(w_down.shape, bf),
        vmem(u_up.shape, bf), vmem(v_up.shape, bf), vmem(u_down.shape, bf), vmem(v_down.shape, bf),
        vmem((tokens, hidden), bf), vmem((tokens, hidden), bf),
        vmem((levels, tokens, 2 * width), bf), vmem((levels, tokens, 2 * width), bf), vmem((tokens, 2 * width), f32),
        vmem((tokens, 2 * rank), f32), vmem((tokens, 2 * rank), bf), vmem((tokens, 2 * rank), bf),
        vmem((tokens, 2 * rank), bf), vmem((tokens, 2 * rank), bf), vmem((tokens, 2 * rank), bf), vmem((tokens, 2 * rank), bf),
        vmem((2, width, hidden), f32), vmem((2, hidden, width), f32), vmem((tokens, width), bf), vmem((tokens, width), bf),
        vmem((width, rank), f32), vmem((rank, hidden), f32), vmem((hidden, rank), f32), vmem((rank, width), f32),
        vmem((8 * levels, 128), f32), vmem((8 * levels, 128), f32),
        dma(8), dma(levels), dma(levels), dma(levels), dma(levels, CHUNKS), dma(levels), dma(levels, CHUNKS),
        dma(2 * rounds), dma(2 * rounds), dma(2 * rounds), dma(2 * rounds), dma(2 * slabs + 4 + 2 * CHUNKS),
    ]
    smem = pl.BlockSpec(memory_space=pltpu.SMEM)
    hbm = pl.BlockSpec(memory_space=pl.ANY)
    got = pl.pallas_call(
        functools.partial(kernel, rounds),
        in_specs=[smem, smem] + [hbm] * 8,
        out_specs=[hbm] * len(outs),
        out_shape=outs,
        scratch_shapes=scratch,
        compiler_params=pltpu.CompilerParams(vmem_limit_bytes=VMEM_LIMIT, collective_id=0, has_side_effects=True),
        name="sublayer",
    )(mask_up[:, 0], mask_down[:, 0], activations, grad_y, w_up, w_down, u_up, v_up, u_down, v_down)
    return tuple(got[:2]) + tuple(summed_over_dp(g) for g in got[2:])


def solution(mesh):
    acts, rows, columns = P("dp", "mp"), P("mp", None), P(None, "mp")
    up, down = P(None, None, "mp"), P(None, "mp", None)
    return jax.shard_map(
        per_device,
        mesh=mesh,
        in_specs=(acts, up, down, rows, columns, rows, columns, columns, columns, acts),
        out_specs=(acts, acts, up, down, rows, columns, rows, columns),
        check_vma=False,
    )
```

```python
import functools

import jax
import jax.numpy as jnp
from jax import lax
from jax.experimental import pallas as pl
from jax.experimental.pallas import tpu as pltpu
from jax.sharding import PartitionSpec as P

CHUNKS = 4
PIECES = 4
PARTS = 2
AHEAD = 2
AHEAD_AT = (7, 9)
ROWS = 256
COLUMNS = 256
ROOT = 0.7978845608028654
CUBIC = 0.044715
VMEM_LIMIT = 67043328
MESH = pl.DeviceIdType.MESH
EARLY_ORDERS = ((0, 1, 2, 3), (0, 2, 3, 1))
LATE_ORDERS = ((0, 2, 3, 1), (0, 1, 2, 3))
EARLY_ISSUE = ((1, 1, 2), (1, 0, 0), (0, 2, 0), (1, 1, 0), (1, 1, 1), (1, 0, 1), (0, 1, 1), (1, 1, 2), (2, 2, 2))
CHUNK_ISSUE = ((2, 2, 2), (2, 2, 2), (0, 1, 2), (0, 0, 0))
LATE_ISSUE = ((1, 0, 1), (0, 1, 1), (1, 1, 1), (1, 1, 1), (2, 1, 1), (0, 1, 1), (1, 1, 0), (1, 1, 1), (2, 2, 2))


def dot(left, right):
    return jnp.dot(left, right, preferred_element_type=jnp.float32)


def dot_nt(left, right):
    return lax.dot_general(left, right, (((1,), (1,)), ((), ())), preferred_element_type=jnp.float32)


def dot_tn(left, right):
    return lax.dot_general(left, right, (((0,), (0,)), ((), ())), preferred_element_type=jnp.float32)


class Sum:
    def __init__(self, me, part, order, acc, sent, got, held, send_sems, recv_sems, apart):
        self.me, self.part, self.order = me, part, order
        self.acc, self.sent, self.got, self.held = acc, sent, got, held
        self.send_sems, self.recv_sems = send_sems, recv_sems
        self.length = acc.shape[0] // PARTS
        self.base, self.offset = jnp.int32(part * self.length), part * self.length
        self.rounds = len(order)
        self.steps = 2 * self.rounds - 1
        self.landing = acc.shape[0] + part * (self.length >> self.rounds - 1) if apart else None
        self.copy = None

    def bit(self, level):
        return lax.rem(lax.div(self.me, jnp.int32(1 << level)), jnp.int32(2))

    def rows(self, base, length):
        return pl.ds(pl.multiple_of(base, length), length)

    def remote(self, src, dst, step, level):
        self.copy = pltpu.make_async_remote_copy(
            src_ref=src, dst_ref=dst, send_sem=self.send_sems.at[self.part, step], recv_sem=self.recv_sems.at[self.part, step],
            device_id={"mp": partner(self.me, level)}, device_id_type=MESH,
        )
        self.copy.start()

    def landed(self, step, size):
        last = step == self.rounds - 1 and self.landing is not None
        return pl.ds(self.landing if last else self.offset, size)

    def start(self, step):
        if step < self.rounds:
            level = self.order[step]
            last = step == self.rounds - 1
            size = self.length if last else self.length // 2
            base = self.base if last else self.base + (1 - self.bit(level)) * size
            here = pl.ds(self.offset, size)
            self.sent[here, :] = self.acc[self.rows(base, size), :].astype(jnp.bfloat16)
            self.remote(self.sent.at[here], self.got.at[self.landed(step, size)], step, level)
        else:
            mine = self.held.at[self.rows(self.base, self.length)]
            self.remote(mine, mine, step, self.order[self.steps - 1 - step])

    def finish(self, step):
        self.copy.wait()
        if step < self.rounds:
            last = step == self.rounds - 1
            size = self.length if last else self.length // 2
            if not last:
                self.base = self.base + self.bit(self.order[step]) * size
            kept = self.rows(self.base, size)
            total = self.acc[kept, :] + self.got[self.landed(step, size), :].astype(jnp.float32)
            if last:
                self.held[kept, :] = total.astype(jnp.bfloat16)
            else:
                self.acc[kept, :] = total
            self.offset += size
            self.length = size
        else:
            self.base = self.base - self.bit(self.order[self.steps - 1 - step]) * self.length
            self.length *= 2

    def advance(self, step):
        if step > 0:
            self.finish(step - 1)
        if step < self.steps:
            self.start(step)


def partner(me, level):
    step = 1 << level
    bit = lax.rem(lax.div(me, jnp.int32(step)), jnp.int32(2))
    return me + (1 - 2 * bit) * step


def kernel(rounds, mu_ref, md_ref, x_hbm, gy_hbm, wu_hbm, wd_hbm, uu_hbm, vu_hbm, ud_hbm, vd_hbm,
           out_hbm, gx_hbm, gwu_hbm, gwd_hbm, guu_hbm, gvu_hbm, gud_hbm, gvd_hbm,
           xs, wu, wd, uu, vu, ud, vd, hid, gp, put, came, diag, acc, zs, zl, sent, got,
           pre, gh_sum, guu, gvd, mask_mine, mask_theirs,
           load_sems, mask_send, mask_recv, in_send, in_recv, put_send, put_recv, es, er, ls, lr, store_sems):
    slabs, tokens = xs.shape[:2]
    levels = slabs - 1
    width, hidden = wu.shape[1:]
    rank = vu.shape[0]
    chunk = tokens // CHUNKS
    piece = chunk // PIECES
    pieces = CHUNKS * PIECES
    step = min(COLUMNS, hidden)
    me = lax.axis_index("mp")

    loads = []
    for i, (src, dst) in enumerate((
        (x_hbm, xs.at[0, :, pl.ds(0, width)]), (gy_hbm, xs.at[0, :, pl.ds(width, width)]),
        (uu_hbm, uu), (vd_hbm, vd), (wu_hbm, wu), (wd_hbm, wd), (vu_hbm, vu), (ud_hbm, ud),
    )):
        loads.append(pltpu.make_async_copy(src, dst, load_sems.at[i]))
        loads[-1].start()

    barrier = pltpu.get_barrier_semaphore()
    for level in range(rounds):
        pl.semaphore_signal(barrier, inc=1, device_id={"mp": partner(me, level)}, device_id_type=MESH)
    for k in range(levels):
        mask_mine[8 * k:8 * k + 8, :] = jnp.full((8, 128), md_ref[k].astype(jnp.float32))
    pl.semaphore_wait(barrier, rounds)

    def mask_copy(k):
        here = pl.ds(8 * k, 8)
        return pltpu.make_async_remote_copy(
            src_ref=mask_mine.at[here], dst_ref=mask_theirs.at[here], send_sem=mask_send.at[k], recv_sem=mask_recv.at[k],
            device_id={"mp": partner(me, k)}, device_id_type=MESH)

    def input_copy(k, start, length):
        rows = pl.ds(start, length)
        return pltpu.make_async_remote_copy(
            src_ref=xs.at[0, rows], dst_ref=xs.at[k + 1, rows], send_sem=in_send.at[k], recv_sem=in_recv.at[k, lax.div(start, chunk)],
            device_id={"mp": partner(me, k)}, device_id_type=MESH)

    def partial_copy(k, start, length):
        rows = pl.ds(start, length)
        return pltpu.make_async_remote_copy(
            src_ref=put.at[k, rows], dst_ref=came.at[k, rows], send_sem=put_send.at[k], recv_sem=put_recv.at[k, lax.div(start, chunk)],
            device_id={"mp": partner(me, k)}, device_id_type=MESH)

    in_done = [0] * levels
    put_done = [0] * levels

    def issue(copy, done, k, count):
        for i in range(done[k], min(pieces, done[k] + count)):
            copy(k, i * piece, piece).start()
        done[k] = min(pieces, done[k] + count)

    loads[0].wait()
    loads[1].wait()
    for k in range(levels):
        mask_copy(k).start()
    issue(input_copy, in_done, 0, PIECES)
    for k in range(1, levels):
        issue(input_copy, in_done, k, EARLY_ISSUE[0][k - 1])
    loads[2].wait()
    loads[3].wait()

    @pl.loop(0, CHUNKS)
    def _(c):
        rows = pl.ds(pl.multiple_of(c * chunk, chunk), chunk)
        acc[rows, :rank] = dot(xs[0, rows, :width], uu[...])
        acc[rows, rank:] = dot_nt(xs[0, rows, width:], vd[...])

    def sums(rows, start):
        cols = slice(start, start + step)
        v = dot(xs[0, rows, :width], wu[0, :, cols])
        gh = dot_nt(xs[0, rows, width:], wd[0, cols, :])
        for k in range(1, slabs):
            v += dot(xs[k, rows, :width], wu[k, :, cols])
            gh += dot_nt(xs[k, rows, width:], wd[k, cols, :])
        return v, gh

    def sums_ahead(c):
        for k in range(levels):
            input_copy(k, c * chunk, chunk).wait_recv()

        @pl.loop(0, chunk // ROWS)
        def _(r):
            rows = pl.ds(pl.multiple_of(c * chunk + r * ROWS, ROWS), ROWS)
            for start in range(0, hidden, step):
                pre[rows, start:start + step], gh_sum[rows, start:start + step] = sums(rows, start)

    tail = tuple(range(levels, rounds))
    early = [
        Sum(me, 0, EARLY_ORDERS[0] + tail, acc, sent, got, zs, es, er, False),
        Sum(me, 1, EARLY_ORDERS[1] + tail, acc, sent, got, zs, es, er, False),
    ]
    for s in range(2 * rounds):
        for part in early:
            part.advance(s)
        if s == 0:
            issue(input_copy, in_done, 0, pieces)
        elif s < len(EARLY_ISSUE):
            for k in range(1, levels):
                issue(input_copy, in_done, k, EARLY_ISSUE[s][k - 1])
        if s == 0:
            loads[4].wait()
            for k in range(levels):
                wu[k + 1] = (wu[k + 1].astype(jnp.float32) * mu_ref[k].astype(jnp.float32)).astype(jnp.bfloat16)
        if s == 1:
            loads[5].wait()
            for k in range(levels):
                mask_copy(k).wait()
                row = jnp.concatenate([mask_theirs[8 * k:8 * k + 1, :]] * (width // 128), axis=1)
                wd[k + 1] = (wd[k + 1].astype(jnp.float32) * row).astype(jnp.bfloat16)
        if s == 2:
            loads[6].wait()
            loads[7].wait()
        if s in AHEAD_AT:
            sums_ahead(AHEAD_AT.index(s))
    for k in range(1, levels):
        issue(input_copy, in_done, k, pieces)

    def products(c, chunks, ahead):
        @pl.loop(0, chunk // ROWS)
        def _(r):
            rows = pl.ds(pl.multiple_of(c * chunk + r * ROWS, ROWS), ROWS)
            for start in range(0, hidden, step):
                cols = slice(start, start + step)
                v, gh = (pre[rows, cols], gh_sum[rows, cols]) if ahead else sums(rows, start)
                v += dot(zs[rows, :rank], vu[:, cols])
                gh += dot_nt(zs[rows, rank:], ud[cols, :])
                square = v * v
                half_tanh = 0.5 * jnp.tanh(v * (ROOT + (ROOT * CUBIC) * square))
                gate = 0.5 + half_tanh
                hid[rows, cols] = (v * gate).astype(jnp.bfloat16)
                slope = gate + v * (0.5 - 2.0 * half_tanh * half_tanh) * (ROOT + (3.0 * ROOT * CUBIC) * square)
                gp[rows, cols] = (gh * slope).astype(jnp.bfloat16)
            h = hid[rows, :]
            g = gp[rows, :]
            for k in range(levels):
                put[k, rows, :width] = dot(h, wd[k + 1]).astype(jnp.bfloat16)
                put[k, rows, width:] = dot_nt(g, wu[k + 1]).astype(jnp.bfloat16)
            acc[rows, :rank] = dot(h, ud[...])
            acc[rows, rank:] = dot_nt(g, vu[...])
            diag[rows, :width] = dot(h, wd[0])
            diag[rows, width:] = dot_nt(g, wu[0])

        partial_copy(0, c * chunk, chunk).start()
        for k in range(1, levels):
            for at in chunks:
                first = sum(row[k - 1] for row in CHUNK_ISSUE[:at])

                @pl.when(c == at)
                def _():
                    for i in range(first, first + CHUNK_ISSUE[at][k - 1]):
                        partial_copy(k, i * piece, piece).start()

    @pl.loop(0, AHEAD)
    def _(c):
        products(c, range(AHEAD), True)

    @pl.loop(AHEAD, CHUNKS)
    def _(c):
        for k in range(levels):
            input_copy(k, c * chunk, chunk).wait_recv()
        products(c, range(AHEAD, CHUNKS), False)

    for k in range(levels):
        put_done[k] = pieces if k == 0 else sum(row[k - 1] for row in CHUNK_ISSUE)

    stores = []

    def store(src, dst):
        stores.append(pltpu.make_async_copy(src, dst, store_sems.at[len(stores)]))
        stores[-1].start()
        return stores[-1]

    held = [None, None]
    pending = []

    def slab_grads(k):
        slot = k % 2
        if held[slot]:
            for copy in held[slot]:
                copy.wait()
                pending.remove(copy)
        for start in range(0, width, ROWS):
            stop = min(width, start + ROWS)
            up = dot_tn(xs[k, :, start:stop], gp[...])
            if k:
                up = up * mu_ref[k - 1].astype(jnp.float32)
            pre[slot * width + start:slot * width + stop, :] = up

        @pl.loop(0, hidden // step)
        def _(b):
            cols = pl.ds(pl.multiple_of(b * step, step), step)
            down = dot_tn(hid[:, cols], xs[k, :, width:])
            if k:
                down = down * jnp.concatenate([mask_theirs[8 * k - 8:8 * k - 7, :]] * (width // 128), axis=1)
            gh_sum[cols, slot * width:(slot + 1) * width] = down

        held[slot] = (store(pre.at[pl.ds(slot * width, width)], gwu_hbm.at[k]), store(gh_sum.at[pl.ds(0, hidden), pl.ds(slot * width, width)], gwd_hbm.at[k]))
        pending.extend(held[slot])

    late = [
        Sum(me, 0, LATE_ORDERS[0] + tail, acc, sent, got, zl, ls, lr, True),
        Sum(me, 1, LATE_ORDERS[1] + tail, acc, sent, got, zl, ls, lr, True),
    ]
    for s in range(2 * rounds):
        for part in late:
            part.advance(s)
        if s < len(LATE_ISSUE):
            for k in range(1, levels):
                issue(partial_copy, put_done, k, LATE_ISSUE[s][k - 1])
        if 1 <= s <= slabs:
            slab_grads(s - 1)
        if s == slabs + 1:
            gvu = pre.at[pl.ds(2 * width, rank)]
            gvu[...] = dot_tn(zs[:, :rank], gp[...])
            pending.append(store(gvu, gvu_hbm))
            gud = gh_sum.at[pl.ds(0, hidden), pl.ds(2 * width, rank)]
            gud[...] = dot_tn(hid[...], zs[:, rank:])
            pending.append(store(gud, gud_hbm))
    for k in range(1, levels):
        issue(partial_copy, put_done, k, pieces)

    guu[...] = dot_tn(xs[0, :, :width], zl[:, rank:])
    pending.append(store(guu, guu_hbm))
    gvd[...] = dot_tn(zl[:, :rank], xs[0, :, width:])
    pending.append(store(gvd, gvd_hbm))

    for c in range(CHUNKS):
        rows = pl.ds(c * chunk, chunk)
        out = diag[rows, :width] + dot(zl[rows, :rank], vd[...])
        gx = diag[rows, width:] + dot_nt(zl[rows, rank:], uu[...])
        for k in range(levels):
            partial_copy(k, c * chunk, chunk).wait_recv()
            out = out + came[k, rows, :width].astype(jnp.float32)
            gx = gx + came[k, rows, width:].astype(jnp.float32)
        hid[rows, :width] = out.astype(jnp.bfloat16)
        hid[rows, width:2 * width] = gx.astype(jnp.bfloat16)
        pending.append(store(hid.at[rows, pl.ds(0, width)], out_hbm.at[rows]))
        pending.append(store(hid.at[rows, pl.ds(width, width)], gx_hbm.at[rows]))
    for copy in pending:
        copy.wait()
    for k in range(levels):
        input_copy(k, 0, tokens).wait_send()
        partial_copy(k, 0, tokens).wait_send()


def settle_kernel(count, *refs):
    sources, targets, buffers = refs[:count], refs[count:2 * count], refs[2 * count:3 * count]
    get_sems, set_sems = refs[3 * count:]
    moves = []
    for source, target, buffer in zip(sources, targets, buffers):
        views = [()] if len(source.shape) == 2 else [(i,) for i in range(source.shape[0])]
        for view in views:
            at = lambda ref, view=view: ref.at[view] if view else ref
            i = len(moves)
            moves.append((
                pltpu.make_async_copy(at(source), at(buffer), get_sems.at[i]),
                pltpu.make_async_copy(at(buffer), at(target), set_sems.at[i]),
            ))
    for get, _ in moves:
        get.start()
    for get, put in moves:
        get.wait()
        put.start()
    for _, put in moves:
        put.wait()


def settled(arrays):
    count = len(arrays)
    moves = sum(a.shape[0] if a.ndim == 3 else 1 for a in arrays)
    size = sum(a.size * a.dtype.itemsize for a in arrays)
    hbm = pl.BlockSpec(memory_space=pl.ANY)
    return pl.pallas_call(
        functools.partial(settle_kernel, count),
        in_specs=[hbm] * count,
        out_specs=[hbm] * count,
        out_shape=[jax.ShapeDtypeStruct(a.shape, a.dtype) for a in arrays],
        scratch_shapes=[pltpu.VMEM(a.shape, a.dtype) for a in arrays] + [pltpu.SemaphoreType.DMA((moves,))] * 2,
        compiler_params=pltpu.CompilerParams(vmem_limit_bytes=VMEM_LIMIT),
        cost_estimate=pl.CostEstimate(flops=0, bytes_accessed=2 * size, transcendentals=0),
        name="settle",
    )(*arrays)


def summed_over_dp(array):
    if lax.axis_size("dp") == 1:
        return array
    return lax.psum(array.astype(jnp.bfloat16), "dp").astype(jnp.float32)


def per_device(activations, w_up, w_down, u_up, v_up, u_down, v_down, mask_up, mask_down, grad_y):
    bf, f32 = jnp.bfloat16, jnp.float32
    slabs, width, hidden = w_up.shape
    tokens = activations.shape[0]
    rank = v_up.shape[0]
    levels = slabs - 1
    rounds = lax.axis_size("mp").bit_length() - 1
    vmem = pltpu.VMEM
    dma = lambda *shape: pltpu.SemaphoreType.DMA(shape)
    shape = jax.ShapeDtypeStruct
    outs = [
        shape((tokens, width), bf), shape((tokens, width), bf), shape((slabs, width, hidden), f32), shape((slabs, hidden, width), f32),
        shape((width, rank), f32), shape((rank, hidden), f32), shape((hidden, rank), f32), shape((rank, width), f32),
    ]
    scratch = [
        vmem((slabs, tokens, 2 * width), bf), vmem(w_up.shape, bf), vmem(w_down.shape, bf),
        vmem(u_up.shape, bf), vmem(v_up.shape, bf), vmem(u_down.shape, bf), vmem(v_down.shape, bf),
        vmem((tokens, hidden), bf), vmem((tokens, hidden), bf),
        vmem((levels, tokens, 2 * width), bf), vmem((levels, tokens, 2 * width), bf), vmem((tokens, 2 * width), f32),
        vmem((tokens, 2 * rank), f32), vmem((tokens, 2 * rank), bf), vmem((tokens, 2 * rank), bf),
        vmem((tokens, 2 * rank), bf), vmem((tokens + (tokens >> rounds - 1), 2 * rank), bf),
        vmem((AHEAD * tokens // CHUNKS, hidden), f32), vmem((AHEAD * tokens // CHUNKS, hidden), f32),
        vmem((width, rank), f32), vmem((rank, width), f32),
        vmem((8 * levels, 128), f32), vmem((8 * levels, 128), f32),
        dma(8), dma(levels), dma(levels), dma(levels), dma(levels, CHUNKS), dma(levels), dma(levels, CHUNKS),
        dma(PARTS, 2 * rounds - 1), dma(PARTS, 2 * rounds - 1), dma(PARTS, 2 * rounds - 1), dma(PARTS, 2 * rounds - 1), dma(2 * slabs + 4 + 2 * CHUNKS),
    ]
    smem = pl.BlockSpec(memory_space=pltpu.SMEM)
    hbm = pl.BlockSpec(memory_space=pl.ANY)
    got = pl.pallas_call(
        functools.partial(kernel, rounds),
        in_specs=[smem, smem] + [hbm] * 8,
        out_specs=[hbm] * len(outs),
        out_shape=outs,
        scratch_shapes=scratch,
        compiler_params=pltpu.CompilerParams(vmem_limit_bytes=VMEM_LIMIT, collective_id=0, has_side_effects=True),
        name="sublayer",
    )(mask_up[:, 0], mask_down[:, 0], activations, grad_y, w_up, w_down, u_up, v_up, u_down, v_down)
    got = settled(got)
    return tuple(got[:2]) + tuple(summed_over_dp(g) for g in got[2:])


def solution(mesh):
    acts, rows, columns = P("dp", "mp"), P("mp", None), P(None, "mp")
    up, down = P(None, None, "mp"), P(None, "mp", None)
    return jax.shard_map(
        per_device,
        mesh=mesh,
        in_specs=(acts, up, down, rows, columns, rows, columns, columns, columns, acts),
        out_specs=(acts, acts, up, down, rows, columns, rows, columns),
        check_vma=False,
    )
```

```python
import functools
import math

import jax
import jax.numpy as jnp
from jax import lax
from jax.experimental import pallas as pl
from jax.experimental.pallas import tpu as pltpu
from jax.sharding import PartitionSpec as P

CHUNKS = 4
PIECES = 4
PARTS = 2
AHEAD = 2
AHEAD_AT = (6, 8)
SLOTS = 4
ROWS = 256
COLUMNS = 256
ROOT = 0.7978845608028654
CUBIC = 0.044715
VMEM_LIMIT = 67043328
MESH = pl.DeviceIdType.MESH
EARLY_ORDERS = ((0, 1, 2, 3), (0, 2, 3, 1))
LATE_ORDERS = ((0, 2, 3, 1), (0, 1, 2, 3))
EARLY_ISSUE = ((1, 1, 2), (1, 0, 0), (0, 2, 0), (1, 1, 0), (1, 1, 1), (1, 0, 1), (0, 1, 1), (1, 1, 2), (2, 2, 2))
CHUNK_ISSUE = ((2, 2, 2), (2, 2, 2), (0, 1, 2), (0, 0, 0))
LATE_ISSUE = ((2, 1, 1), (1, 1, 1), (1, 1, 1), (1, 2, 1), (2, 1, 2), (1, 1, 1), (1, 1, 1), (2, 2, 2), (4, 4, 4))


def dot(left, right):
    return jnp.dot(left, right, preferred_element_type=jnp.float32)


def dot_nt(left, right):
    return lax.dot_general(left, right, (((1,), (1,)), ((), ())), preferred_element_type=jnp.float32)


def dot_tn(left, right):
    return lax.dot_general(left, right, (((0,), (0,)), ((), ())), preferred_element_type=jnp.float32)


class Sum:
    def __init__(self, me, part, order, acc, sent, got, held, send_sems, recv_sems, apart):
        self.me, self.part, self.order = me, part, order
        self.acc, self.sent, self.got, self.held = acc, sent, got, held
        self.send_sems, self.recv_sems = send_sems, recv_sems
        self.length = acc.shape[0] // PARTS
        self.base, self.offset = jnp.int32(part * self.length), part * self.length
        self.rounds = len(order)
        self.steps = 2 * self.rounds - 1
        self.landing = acc.shape[0] + part * (self.length >> self.rounds - 1) if apart else None
        self.copy = None

    def bit(self, level):
        return lax.rem(lax.div(self.me, jnp.int32(1 << level)), jnp.int32(2))

    def rows(self, base, length):
        return pl.ds(pl.multiple_of(base, length), length)

    def remote(self, src, dst, step, level):
        self.copy = pltpu.make_async_remote_copy(
            src_ref=src, dst_ref=dst, send_sem=self.send_sems.at[self.part, step], recv_sem=self.recv_sems.at[self.part, step],
            device_id={"mp": partner(self.me, level)}, device_id_type=MESH,
        )
        self.copy.start()

    def landed(self, step, size):
        last = step == self.rounds - 1 and self.landing is not None
        return pl.ds(self.landing if last else self.offset, size)

    def start(self, step):
        if step < self.rounds:
            level = self.order[step]
            last = step == self.rounds - 1
            size = self.length if last else self.length // 2
            base = self.base if last else self.base + (1 - self.bit(level)) * size
            here = pl.ds(self.offset, size)
            self.sent[here, :] = self.acc[self.rows(base, size), :].astype(jnp.bfloat16)
            self.remote(self.sent.at[here], self.got.at[self.landed(step, size)], step, level)
        else:
            mine = self.held.at[self.rows(self.base, self.length)]
            self.remote(mine, mine, step, self.order[self.steps - 1 - step])

    def finish(self, step):
        self.copy.wait()
        if step < self.rounds:
            last = step == self.rounds - 1
            size = self.length if last else self.length // 2
            if not last:
                self.base = self.base + self.bit(self.order[step]) * size
            kept = self.rows(self.base, size)
            total = self.acc[kept, :] + self.got[self.landed(step, size), :].astype(jnp.float32)
            if last:
                self.held[kept, :] = total.astype(jnp.bfloat16)
            else:
                self.acc[kept, :] = total
            self.offset += size
            self.length = size
        else:
            self.base = self.base - self.bit(self.order[self.steps - 1 - step]) * self.length
            self.length *= 2

    def advance(self, step):
        if step > 0:
            self.finish(step - 1)
        if step < self.steps:
            self.start(step)


def partner(me, level):
    step = 1 << level
    bit = lax.rem(lax.div(me, jnp.int32(step)), jnp.int32(2))
    return me + (1 - 2 * bit) * step


def kernel(rounds, mu_ref, md_ref, x_hbm, gy_hbm, wu_hbm, wd_hbm, uu_hbm, vu_hbm, ud_hbm, vd_hbm,
           pre, gh_sum, acc, hid, guu, gvd, gvu, gud,
           xs, wu, wd, uu, vu, ud, vd, gp, put, came, diag, zs, zl, sent, got, mask_mine, mask_theirs,
           load_sems, mask_send, mask_recv, in_send, in_recv, put_send, put_recv, es, er, ls, lr):
    slabs, tokens = xs.shape[:2]
    levels = slabs - 1
    width, hidden = wu.shape[1:]
    rank = vu.shape[0]
    chunk = tokens // CHUNKS
    piece = chunk // PIECES
    pieces = CHUNKS * PIECES
    step = min(COLUMNS, hidden)
    me = lax.axis_index("mp")

    loads = []
    for i, (src, dst) in enumerate((
        (x_hbm, xs.at[0, :, pl.ds(0, width)]), (gy_hbm, xs.at[0, :, pl.ds(width, width)]),
        (uu_hbm, uu), (vd_hbm, vd), (wu_hbm, wu), (wd_hbm, wd), (vu_hbm, vu), (ud_hbm, ud),
    )):
        loads.append(pltpu.make_async_copy(src, dst, load_sems.at[i]))
        loads[-1].start()

    barrier = pltpu.get_barrier_semaphore()
    for level in range(rounds):
        pl.semaphore_signal(barrier, inc=1, device_id={"mp": partner(me, level)}, device_id_type=MESH)
    for k in range(levels):
        mask_mine[8 * k:8 * k + 8, :] = jnp.full((8, 128), md_ref[k].astype(jnp.float32))
    pl.semaphore_wait(barrier, rounds)

    def mask_copy(k):
        here = pl.ds(8 * k, 8)
        return pltpu.make_async_remote_copy(
            src_ref=mask_mine.at[here], dst_ref=mask_theirs.at[here], send_sem=mask_send.at[k], recv_sem=mask_recv.at[k],
            device_id={"mp": partner(me, k)}, device_id_type=MESH)

    def input_copy(k, start, length):
        rows = pl.ds(start, length)
        return pltpu.make_async_remote_copy(
            src_ref=xs.at[0, rows], dst_ref=xs.at[k + 1, rows], send_sem=in_send.at[k], recv_sem=in_recv.at[k, lax.div(start, chunk)],
            device_id={"mp": partner(me, k)}, device_id_type=MESH)

    def partial_copy(k, start, length):
        rows = pl.ds(start, length)
        return pltpu.make_async_remote_copy(
            src_ref=put.at[k, rows], dst_ref=came.at[k, rows], send_sem=put_send.at[k], recv_sem=put_recv.at[k, lax.div(start, chunk)],
            device_id={"mp": partner(me, k)}, device_id_type=MESH)

    in_done = [0] * levels
    put_done = [0] * levels

    def issue(copy, done, k, count):
        for i in range(done[k], min(pieces, done[k] + count)):
            copy(k, i * piece, piece).start()
        done[k] = min(pieces, done[k] + count)

    loads[0].wait()
    loads[1].wait()
    for k in range(levels):
        mask_copy(k).start()
    issue(input_copy, in_done, 0, PIECES)
    for k in range(1, levels):
        issue(input_copy, in_done, k, EARLY_ISSUE[0][k - 1])
    loads[2].wait()
    loads[3].wait()

    @pl.loop(0, CHUNKS)
    def _(c):
        rows = pl.ds(pl.multiple_of(c * chunk, chunk), chunk)
        acc[rows, :rank] = dot(xs[0, rows, :width], uu[...])
        acc[rows, rank:] = dot_nt(xs[0, rows, width:], vd[...])

    def sums(rows, start):
        cols = slice(start, start + step)
        v = dot(xs[0, rows, :width], wu[0, :, cols])
        gh = dot_nt(xs[0, rows, width:], wd[0, cols, :])
        for k in range(1, slabs):
            v += dot(xs[k, rows, :width], wu[k, :, cols])
            gh += dot_nt(xs[k, rows, width:], wd[k, cols, :])
        return v, gh

    def sums_ahead(c):
        for k in range(levels):
            input_copy(k, c * chunk, chunk).wait_recv()

        @pl.loop(0, chunk // ROWS)
        def _(r):
            rows = pl.ds(pl.multiple_of(c * chunk + r * ROWS, ROWS), ROWS)
            for start in range(0, hidden, step):
                pre[rows, start:start + step], gh_sum[rows, start:start + step] = sums(rows, start)

    tail = tuple(range(levels, rounds))
    early = [
        Sum(me, 0, EARLY_ORDERS[0] + tail, acc, sent, got, zs, es, er, False),
        Sum(me, 1, EARLY_ORDERS[1] + tail, acc, sent, got, zs, es, er, False),
    ]
    for s in range(2 * rounds):
        for part in early:
            part.advance(s)
        if s == 0:
            issue(input_copy, in_done, 0, pieces)
        elif s < len(EARLY_ISSUE):
            for k in range(1, levels):
                issue(input_copy, in_done, k, EARLY_ISSUE[s][k - 1])
        if s == 0:
            loads[4].wait()
            for k in range(levels):
                wu[k + 1] = (wu[k + 1].astype(jnp.float32) * mu_ref[k].astype(jnp.float32)).astype(jnp.bfloat16)
        if s == 1:
            loads[5].wait()
            for k in range(levels):
                mask_copy(k).wait()
                row = jnp.concatenate([mask_theirs[8 * k:8 * k + 1, :]] * (width // 128), axis=1)
                wd[k + 1] = (wd[k + 1].astype(jnp.float32) * row).astype(jnp.bfloat16)
        if s == 2:
            loads[6].wait()
            loads[7].wait()
        if s in AHEAD_AT:
            sums_ahead(AHEAD_AT.index(s))
    for k in range(1, levels):
        issue(input_copy, in_done, k, pieces)

    def products(c, chunks, ahead):
        @pl.loop(0, chunk // ROWS)
        def _(r):
            rows = pl.ds(pl.multiple_of(c * chunk + r * ROWS, ROWS), ROWS)
            for start in range(0, hidden, step):
                cols = slice(start, start + step)
                v, gh = (pre[rows, cols], gh_sum[rows, cols]) if ahead else sums(rows, start)
                v += dot(zs[rows, :rank], vu[:, cols])
                gh += dot_nt(zs[rows, rank:], ud[cols, :])
                square = v * v
                half_tanh = 0.5 * jnp.tanh(v * (ROOT + (ROOT * CUBIC) * square))
                gate = 0.5 + half_tanh
                hid[rows, cols] = (v * gate).astype(jnp.bfloat16)
                slope = gate + v * (0.5 - 2.0 * half_tanh * half_tanh) * (ROOT + (3.0 * ROOT * CUBIC) * square)
                gp[rows, cols] = (gh * slope).astype(jnp.bfloat16)
            h = hid[rows, :]
            g = gp[rows, :]
            for k in range(levels):
                put[k, rows, :width] = dot(h, wd[k + 1]).astype(jnp.bfloat16)
                put[k, rows, width:] = dot_nt(g, wu[k + 1]).astype(jnp.bfloat16)
            acc[rows, :rank] = dot(h, ud[...])
            acc[rows, rank:] = dot_nt(g, vu[...])
            diag[rows, :width] = dot(h, wd[0])
            diag[rows, width:] = dot_nt(g, wu[0])

        partial_copy(0, c * chunk, chunk).start()
        for k in range(1, levels):
            for at in chunks:
                first = sum(row[k - 1] for row in CHUNK_ISSUE[:at])

                @pl.when(c == at)
                def _():
                    for i in range(first, first + CHUNK_ISSUE[at][k - 1]):
                        partial_copy(k, i * piece, piece).start()

    @pl.loop(0, AHEAD)
    def _(c):
        products(c, range(AHEAD), True)

    @pl.loop(AHEAD, CHUNKS)
    def _(c):
        for k in range(levels):
            input_copy(k, c * chunk, chunk).wait_recv()
        products(c, range(AHEAD, CHUNKS), False)

    for k in range(levels):
        put_done[k] = pieces if k == 0 else sum(row[k - 1] for row in CHUNK_ISSUE)

    def slab_grads(k):
        for start in range(0, width, ROWS):
            stop = min(width, start + ROWS)
            up = dot_tn(xs[k, :, start:stop], gp[...])
            if k:
                up = up * mu_ref[k - 1].astype(jnp.float32)
            if k < SLOTS:
                pre[k * width + start:k * width + stop, :] = up
            else:
                for j in range(hidden // (2 * rank)):
                    base = hidden + j * width
                    acc[base + start:base + stop, :] = up[:, j * 2 * rank:(j + 1) * 2 * rank]

        @pl.loop(0, hidden // step)
        def _(b):
            cols = pl.ds(pl.multiple_of(b * step, step), step)
            down = dot_tn(hid[:, cols], xs[k, :, width:])
            if k:
                down = down * jnp.concatenate([mask_theirs[8 * k - 8:8 * k - 7, :]] * (width // 128), axis=1)
            if k < SLOTS:
                gh_sum[cols, k * width:(k + 1) * width] = down
            else:
                acc[cols, :width] = down

    def rank_grads():
        gvu[...] = dot_tn(zs[:, :rank], gp[...])
        gud[...] = dot_tn(hid[...], zs[:, rank:])

    late = [
        Sum(me, 0, LATE_ORDERS[0] + tail, acc, sent, got, zl, ls, lr, True),
        Sum(me, 1, LATE_ORDERS[1] + tail, acc, sent, got, zl, ls, lr, True),
    ]
    for s in range(2 * rounds):
        for part in late:
            part.advance(s)
        if s < len(LATE_ISSUE):
            for k in range(1, levels):
                issue(partial_copy, put_done, k, LATE_ISSUE[s][k - 1])
        if s < SLOTS:
            slab_grads(s)
        if s == rounds:
            rank_grads()
        if s == rounds + 1:
            slab_grads(SLOTS)
    for k in range(1, levels):
        issue(partial_copy, put_done, k, pieces)

    guu[...] = dot_tn(xs[0, :, :width], zl[:, rank:])
    gvd[...] = dot_tn(zl[:, :rank], xs[0, :, width:])

    for c in range(CHUNKS):
        rows = pl.ds(c * chunk, chunk)
        out = diag[rows, :width] + dot(zl[rows, :rank], vd[...])
        gx = diag[rows, width:] + dot_nt(zl[rows, rank:], uu[...])
        for k in range(levels):
            partial_copy(k, c * chunk, chunk).wait_recv()
            out = out + came[k, rows, :width].astype(jnp.float32)
            gx = gx + came[k, rows, width:].astype(jnp.float32)
        hid[rows, :width] = out.astype(jnp.bfloat16)
        hid[rows, width:2 * width] = gx.astype(jnp.bfloat16)
    for k in range(levels):
        input_copy(k, 0, tokens).wait_send()
        partial_copy(k, 0, tokens).wait_send()


def settle_kernel(pre, gh_sum, acc, hid, guu, gvd, gvu, gud, out, gx, gwu, gwd, guu_out, gvu_out, gud_out, gvd_out, sems):
    slabs, width, hidden = gwu.shape
    block = acc.shape[1]
    pairs = []
    for k in range(SLOTS):
        pairs.append((pre.at[pl.ds(k * width, width)], gwu.at[k]))
        pairs.append((gh_sum.at[pl.ds(0, hidden), pl.ds(k * width, width)], gwd.at[k]))
    for j in range(hidden // block):
        pairs.append((acc.at[pl.ds(hidden + j * width, width)], gwu.at[SLOTS, :, pl.ds(j * block, block)]))
    pairs.append((acc.at[pl.ds(0, hidden), pl.ds(0, width)], gwd.at[SLOTS]))
    pairs.append((hid.at[:, pl.ds(0, width)], out))
    pairs.append((hid.at[:, pl.ds(width, width)], gx))
    pairs.append((guu, guu_out))
    pairs.append((gvd, gvd_out))
    pairs.append((gvu, gvu_out))
    pairs.append((gud, gud_out))
    puts = [pltpu.make_async_copy(src, dst, sems.at[i]) for i, (src, dst) in enumerate(pairs)]
    for copy in puts:
        copy.start()
    for copy in puts:
        copy.wait()


def settled(got, outs):
    width, hidden = outs[2].shape[1:]
    copies = 2 * SLOTS + hidden // got[2].shape[1] + 7
    size = sum(a.size * a.dtype.itemsize for a in outs)
    hbm, vmem = pl.BlockSpec(memory_space=pl.ANY), pl.BlockSpec(memory_space=pltpu.VMEM)
    return pl.pallas_call(
        settle_kernel,
        in_specs=[vmem] * len(got),
        out_specs=[hbm] * len(outs),
        out_shape=outs,
        scratch_shapes=[pltpu.SemaphoreType.DMA((copies,))],
        compiler_params=pltpu.CompilerParams(vmem_limit_bytes=1024 * 1024),
        cost_estimate=pl.CostEstimate(flops=0, bytes_accessed=size, transcendentals=0),
        name="settle",
    )(*got)


def summed_over_dp(array):
    if lax.axis_size("dp") == 1:
        return array
    return lax.psum(array.astype(jnp.bfloat16), "dp").astype(jnp.float32)


def per_device(activations, w_up, w_down, u_up, v_up, u_down, v_down, mask_up, mask_down, grad_y):
    bf, f32 = jnp.bfloat16, jnp.float32
    slabs, width, hidden = w_up.shape
    tokens = activations.shape[0]
    rank = v_up.shape[0]
    levels = slabs - 1
    rounds = lax.axis_size("mp").bit_length() - 1
    vmem = pltpu.VMEM
    dma = lambda *shape: pltpu.SemaphoreType.DMA(shape)
    shape = jax.ShapeDtypeStruct
    outs = [
        shape((tokens, width), bf), shape((tokens, width), bf), shape((slabs, width, hidden), f32), shape((slabs, hidden, width), f32),
        shape((width, rank), f32), shape((rank, hidden), f32), shape((hidden, rank), f32), shape((rank, width), f32),
    ]
    scratch = [
        vmem((slabs, tokens, 2 * width), bf), vmem(w_up.shape, bf), vmem(w_down.shape, bf),
        vmem(u_up.shape, bf), vmem(v_up.shape, bf), vmem(u_down.shape, bf), vmem(v_down.shape, bf),
        vmem((tokens, hidden), bf),
        vmem((levels, tokens, 2 * width), bf), vmem((levels, tokens, 2 * width), bf), vmem((tokens, 2 * width), f32),
        vmem((tokens, 2 * rank), bf), vmem((tokens, 2 * rank), bf),
        vmem((tokens, 2 * rank), bf), vmem((tokens + (tokens >> rounds - 1), 2 * rank), bf),
        vmem((8 * levels, 128), f32), vmem((8 * levels, 128), f32),
        dma(8), dma(levels), dma(levels), dma(levels), dma(levels, CHUNKS), dma(levels), dma(levels, CHUNKS),
        dma(PARTS, 2 * rounds - 1), dma(PARTS, 2 * rounds - 1), dma(PARTS, 2 * rounds - 1), dma(PARTS, 2 * rounds - 1),
    ]
    left = [
        ((AHEAD * tokens // CHUNKS, hidden), f32), ((AHEAD * tokens // CHUNKS, hidden), f32), ((tokens, 2 * rank), f32),
        ((tokens, hidden), bf), ((width, rank), f32), ((rank, width), f32), ((rank, hidden), f32), ((hidden, rank), f32),
    ]
    taken = sum(math.prod(dims) * jnp.dtype(dtype).itemsize for dims, dtype in left)
    smem = pl.BlockSpec(memory_space=pltpu.SMEM)
    hbm = pl.BlockSpec(memory_space=pl.ANY)
    got = pl.pallas_call(
        functools.partial(kernel, rounds),
        in_specs=[smem, smem] + [hbm] * 8,
        out_specs=[pl.BlockSpec(memory_space=vmem)] * len(left),
        out_shape=[vmem(*spec) for spec in left],
        scratch_shapes=scratch,
        compiler_params=pltpu.CompilerParams(vmem_limit_bytes=VMEM_LIMIT - taken, collective_id=0, has_side_effects=True),
        name="sublayer",
    )(mask_up[:, 0], mask_down[:, 0], activations, grad_y, w_up, w_down, u_up, v_up, u_down, v_down)
    got = settled(got, outs)
    return tuple(got[:2]) + tuple(summed_over_dp(g) for g in got[2:])


def solution(mesh):
    acts, rows, columns = P("dp", "mp"), P("mp", None), P(None, "mp")
    up, down = P(None, None, "mp"), P(None, "mp", None)
    return jax.shard_map(
        per_device,
        mesh=mesh,
        in_specs=(acts, up, down, rows, columns, rows, columns, columns, columns, acts),
        out_specs=(acts, acts, up, down, rows, columns, rows, columns),
        check_vma=False,
    )
```

```python
import functools
import math

import jax
import jax.numpy as jnp
from jax import lax
from jax.experimental import pallas as pl
from jax.experimental.pallas import tpu as pltpu
from jax.sharding import PartitionSpec as P

CHUNKS = 4
PIECES = 4
PARTS = 2
AHEAD = 2
AHEAD_AT = (6, 8)
SLOTS = 4
FIRST_SLAB = 1
ROWS = 256
COLUMNS = 256
ROOT = 0.7978845608028654
CUBIC = 0.044715
VMEM_LIMIT = 67043328
MESH = pl.DeviceIdType.MESH
EARLY_ORDERS = ((0, 1, 2, 3), (0, 2, 3, 1))
LATE_ORDERS = ((0, 2, 3, 1), (0, 1, 2, 3))
EARLY_ISSUE = ((2, 1, 2), (1, 0, 1), (0, 2, 0), (1, 1, 1), (1, 1, 1), (1, 1, 1), (1, 1, 1), (1, 1, 1), (2, 2, 2))
CHUNK_ISSUE = ((2, 2, 2), (2, 2, 2), (0, 1, 2), (0, 0, 0))
LATE_ISSUE = ((2, 1, 1), (1, 1, 1), (1, 1, 1), (1, 2, 1), (2, 1, 2), (1, 1, 1), (1, 1, 1), (2, 2, 2), (4, 4, 4))


def dot(left, right):
    return jnp.dot(left, right, preferred_element_type=jnp.float32)


def dot_nt(left, right):
    return lax.dot_general(left, right, (((1,), (1,)), ((), ())), preferred_element_type=jnp.float32)


def dot_tn(left, right):
    return lax.dot_general(left, right, (((0,), (0,)), ((), ())), preferred_element_type=jnp.float32)


class Sum:
    def __init__(self, me, part, order, acc, sent, got, held, send_sems, recv_sems, apart):
        self.me, self.part, self.order = me, part, order
        self.acc, self.sent, self.got, self.held = acc, sent, got, held
        self.send_sems, self.recv_sems = send_sems, recv_sems
        self.length = acc.shape[0] // PARTS
        self.base, self.offset = jnp.int32(part * self.length), part * self.length
        self.rounds = len(order)
        self.steps = 2 * self.rounds - 1
        self.landing = acc.shape[0] + part * (self.length >> self.rounds - 1) if apart else None
        self.copy = None

    def bit(self, level):
        return lax.rem(lax.div(self.me, jnp.int32(1 << level)), jnp.int32(2))

    def rows(self, base, length):
        return pl.ds(pl.multiple_of(base, length), length)

    def remote(self, src, dst, step, level):
        self.copy = pltpu.make_async_remote_copy(
            src_ref=src, dst_ref=dst, send_sem=self.send_sems.at[self.part, step], recv_sem=self.recv_sems.at[self.part, step],
            device_id={"mp": partner(self.me, level)}, device_id_type=MESH,
        )
        self.copy.start()

    def landed(self, step, size):
        last = step == self.rounds - 1 and self.landing is not None
        return pl.ds(self.landing if last else self.offset, size)

    def start(self, step):
        if step < self.rounds:
            level = self.order[step]
            last = step == self.rounds - 1
            size = self.length if last else self.length // 2
            base = self.base if last else self.base + (1 - self.bit(level)) * size
            here = pl.ds(self.offset, size)
            self.sent[here, :] = self.acc[self.rows(base, size), :].astype(jnp.bfloat16)
            self.remote(self.sent.at[here], self.got.at[self.landed(step, size)], step, level)
        else:
            mine = self.held.at[self.rows(self.base, self.length)]
            self.remote(mine, mine, step, self.order[self.steps - 1 - step])

    def finish(self, step):
        self.copy.wait()
        if step < self.rounds:
            last = step == self.rounds - 1
            size = self.length if last else self.length // 2
            if not last:
                self.base = self.base + self.bit(self.order[step]) * size
            kept = self.rows(self.base, size)
            total = self.acc[kept, :] + self.got[self.landed(step, size), :].astype(jnp.float32)
            if last:
                self.held[kept, :] = total.astype(jnp.bfloat16)
            else:
                self.acc[kept, :] = total
            self.offset += size
            self.length = size
        else:
            self.base = self.base - self.bit(self.order[self.steps - 1 - step]) * self.length
            self.length *= 2

    def advance(self, step):
        if step > 0:
            self.finish(step - 1)
        if step < self.steps:
            self.start(step)


def partner(me, level):
    step = 1 << level
    bit = lax.rem(lax.div(me, jnp.int32(step)), jnp.int32(2))
    return me + (1 - 2 * bit) * step


def kernel(rounds, mu_ref, md_ref, x_hbm, gy_hbm, wu_hbm, wd_hbm, uu_hbm, vu_hbm, ud_hbm, vd_hbm,
           pre, gh_sum, acc, hid, guu, gvd, gvu, gud,
           xs, wu, wd, uu, vu, ud, vd, gp, put, came, diag, zs, zl, sent, got, mask_mine, mask_theirs,
           load_sems, mask_send, mask_recv, in_send, in_recv, put_send, put_recv, es, er, ls, lr):
    slabs, tokens = xs.shape[:2]
    levels = slabs - 1
    width, hidden = wu.shape[1:]
    rank = vu.shape[0]
    chunk = tokens // CHUNKS
    piece = chunk // PIECES
    pieces = CHUNKS * PIECES
    step = min(COLUMNS, hidden)
    me = lax.axis_index("mp")

    loads = []
    for i, (src, dst) in enumerate((
        (x_hbm, xs.at[0, :, pl.ds(0, width)]), (gy_hbm, xs.at[0, :, pl.ds(width, width)]),
        (uu_hbm, uu), (vd_hbm, vd), (wu_hbm, wu), (wd_hbm, wd), (vu_hbm, vu), (ud_hbm, ud),
    )):
        loads.append(pltpu.make_async_copy(src, dst, load_sems.at[i]))
        loads[-1].start()

    barrier = pltpu.get_barrier_semaphore()
    for level in range(rounds):
        pl.semaphore_signal(barrier, inc=1, device_id={"mp": partner(me, level)}, device_id_type=MESH)
    for k in range(levels):
        mask_mine[8 * k:8 * k + 8, :] = jnp.full((8, 128), md_ref[k].astype(jnp.float32))
    pl.semaphore_wait(barrier, rounds)

    def mask_copy(k):
        here = pl.ds(8 * k, 8)
        return pltpu.make_async_remote_copy(
            src_ref=mask_mine.at[here], dst_ref=mask_theirs.at[here], send_sem=mask_send.at[k], recv_sem=mask_recv.at[k],
            device_id={"mp": partner(me, k)}, device_id_type=MESH)

    def input_copy(k, start, length):
        rows = pl.ds(start, length)
        return pltpu.make_async_remote_copy(
            src_ref=xs.at[0, rows], dst_ref=xs.at[k + 1, rows], send_sem=in_send.at[k], recv_sem=in_recv.at[k, lax.div(start, chunk)],
            device_id={"mp": partner(me, k)}, device_id_type=MESH)

    def partial_copy(k, start, length):
        rows = pl.ds(start, length)
        return pltpu.make_async_remote_copy(
            src_ref=put.at[k, rows], dst_ref=came.at[k, rows], send_sem=put_send.at[k], recv_sem=put_recv.at[k, lax.div(start, chunk)],
            device_id={"mp": partner(me, k)}, device_id_type=MESH)

    in_done = [0] * levels
    put_done = [0] * levels

    def issue(copy, done, k, count):
        for i in range(done[k], min(pieces, done[k] + count)):
            copy(k, i * piece, piece).start()
        done[k] = min(pieces, done[k] + count)

    loads[0].wait()
    loads[1].wait()
    for k in range(levels):
        mask_copy(k).start()
    issue(input_copy, in_done, 0, PIECES)
    for k in range(1, levels):
        issue(input_copy, in_done, k, EARLY_ISSUE[0][k - 1])
    loads[2].wait()
    loads[3].wait()

    @pl.loop(0, CHUNKS)
    def _(c):
        rows = pl.ds(pl.multiple_of(c * chunk, chunk), chunk)
        acc[rows, :rank] = dot(xs[0, rows, :width], uu[...])
        acc[rows, rank:] = dot_nt(xs[0, rows, width:], vd[...])

    def sums(rows, start):
        cols = slice(start, start + step)
        v = dot(xs[0, rows, :width], wu[0, :, cols])
        gh = dot_nt(xs[0, rows, width:], wd[0, cols, :])
        for k in range(1, slabs):
            v += dot(xs[k, rows, :width], wu[k, :, cols])
            gh += dot_nt(xs[k, rows, width:], wd[k, cols, :])
        return v, gh

    def sums_ahead(c):
        for k in range(levels):
            input_copy(k, c * chunk, chunk).wait_recv()

        @pl.loop(0, chunk // ROWS)
        def _(r):
            rows = pl.ds(pl.multiple_of(c * chunk + r * ROWS, ROWS), ROWS)
            for start in range(0, hidden, step):
                pre[rows, start:start + step], gh_sum[rows, start:start + step] = sums(rows, start)

    tail = tuple(range(levels, rounds))
    early = [
        Sum(me, 0, EARLY_ORDERS[0] + tail, acc, sent, got, zs, es, er, False),
        Sum(me, 1, EARLY_ORDERS[1] + tail, acc, sent, got, zs, es, er, False),
    ]
    for s in range(2 * rounds):
        for part in early:
            part.advance(s)
        if s == 0:
            issue(input_copy, in_done, 0, pieces)
        elif s < len(EARLY_ISSUE):
            for k in range(1, levels):
                issue(input_copy, in_done, k, EARLY_ISSUE[s][k - 1])
        if s == 0:
            loads[4].wait()
            for k in range(levels):
                wu[k + 1] = (wu[k + 1].astype(jnp.float32) * mu_ref[k].astype(jnp.float32)).astype(jnp.bfloat16)
        if s == 1:
            loads[5].wait()
            for k in range(levels):
                mask_copy(k).wait()
                row = jnp.concatenate([mask_theirs[8 * k:8 * k + 1, :]] * (width // 128), axis=1)
                wd[k + 1] = (wd[k + 1].astype(jnp.float32) * row).astype(jnp.bfloat16)
        if s == 2:
            loads[6].wait()
            loads[7].wait()
        if s in AHEAD_AT:
            sums_ahead(AHEAD_AT.index(s))
    for k in range(1, levels):
        issue(input_copy, in_done, k, pieces)

    def products(c, chunks, ahead):
        @pl.loop(0, chunk // ROWS)
        def _(r):
            rows = pl.ds(pl.multiple_of(c * chunk + r * ROWS, ROWS), ROWS)
            for start in range(0, hidden, step):
                cols = slice(start, start + step)
                v, gh = (pre[rows, cols], gh_sum[rows, cols]) if ahead else sums(rows, start)
                v += dot(zs[rows, :rank], vu[:, cols])
                gh += dot_nt(zs[rows, rank:], ud[cols, :])
                square = v * v
                half_tanh = 0.5 * jnp.tanh(v * (ROOT + (ROOT * CUBIC) * square))
                gate = 0.5 + half_tanh
                hid[rows, cols] = (v * gate).astype(jnp.bfloat16)
                slope = gate + v * (0.5 - 2.0 * half_tanh * half_tanh) * (ROOT + (3.0 * ROOT * CUBIC) * square)
                gp[rows, cols] = (gh * slope).astype(jnp.bfloat16)
            h = hid[rows, :]
            g = gp[rows, :]
            for k in range(levels):
                put[k, rows, :width] = dot(h, wd[k + 1]).astype(jnp.bfloat16)
                put[k, rows, width:] = dot_nt(g, wu[k + 1]).astype(jnp.bfloat16)
            acc[rows, :rank] = dot(h, ud[...])
            acc[rows, rank:] = dot_nt(g, vu[...])
            diag[rows, :width] = dot(h, wd[0])
            diag[rows, width:] = dot_nt(g, wu[0])

        partial_copy(0, c * chunk, chunk).start()
        for k in range(1, levels):
            for at in chunks:
                first = sum(row[k - 1] for row in CHUNK_ISSUE[:at])

                @pl.when(c == at)
                def _():
                    for i in range(first, first + CHUNK_ISSUE[at][k - 1]):
                        partial_copy(k, i * piece, piece).start()

    @pl.loop(0, AHEAD)
    def _(c):
        products(c, range(AHEAD), True)

    @pl.loop(AHEAD, CHUNKS)
    def _(c):
        for k in range(levels):
            input_copy(k, c * chunk, chunk).wait_recv()
        products(c, range(AHEAD, CHUNKS), False)

    for k in range(levels):
        put_done[k] = pieces if k == 0 else sum(row[k - 1] for row in CHUNK_ISSUE)

    def slab_grads(k):
        for start in range(0, width, ROWS):
            stop = min(width, start + ROWS)
            up = dot_tn(xs[k, :, start:stop], gp[...])
            if k:
                up = up * mu_ref[k - 1].astype(jnp.float32)
            if k < SLOTS:
                pre[k * width + start:k * width + stop, :] = up
            else:
                for j in range(hidden // (2 * rank)):
                    base = hidden + j * width
                    acc[base + start:base + stop, :] = up[:, j * 2 * rank:(j + 1) * 2 * rank]

        @pl.loop(0, hidden // step)
        def _(b):
            cols = pl.ds(pl.multiple_of(b * step, step), step)
            down = dot_tn(hid[:, cols], xs[k, :, width:])
            if k:
                down = down * jnp.concatenate([mask_theirs[8 * k - 8:8 * k - 7, :]] * (width // 128), axis=1)
            if k < SLOTS:
                gh_sum[cols, k * width:(k + 1) * width] = down
            else:
                acc[cols, :width] = down

    def rank_grads():
        gvu[...] = dot_tn(zs[:, :rank], gp[...])
        gud[...] = dot_tn(hid[...], zs[:, rank:])

    late = [
        Sum(me, 0, LATE_ORDERS[0] + tail, acc, sent, got, zl, ls, lr, True),
        Sum(me, 1, LATE_ORDERS[1] + tail, acc, sent, got, zl, ls, lr, True),
    ]
    for s in range(2 * rounds):
        for part in late:
            part.advance(s)
        if s < len(LATE_ISSUE):
            for k in range(1, levels):
                issue(partial_copy, put_done, k, LATE_ISSUE[s][k - 1])
        if FIRST_SLAB <= s < FIRST_SLAB + SLOTS:
            slab_grads(s - FIRST_SLAB)
        if s == rounds + 2:
            rank_grads()
        if s == rounds + 1:
            slab_grads(SLOTS)
    for k in range(1, levels):
        issue(partial_copy, put_done, k, pieces)

    guu[...] = dot_tn(xs[0, :, :width], zl[:, rank:])
    gvd[...] = dot_tn(zl[:, :rank], xs[0, :, width:])

    for c in range(CHUNKS):
        rows = pl.ds(c * chunk, chunk)
        out = diag[rows, :width] + dot(zl[rows, :rank], vd[...])
        gx = diag[rows, width:] + dot_nt(zl[rows, rank:], uu[...])
        for k in range(levels):
            partial_copy(k, c * chunk, chunk).wait_recv()
            out = out + came[k, rows, :width].astype(jnp.float32)
            gx = gx + came[k, rows, width:].astype(jnp.float32)
        hid[rows, :width] = out.astype(jnp.bfloat16)
        hid[rows, width:2 * width] = gx.astype(jnp.bfloat16)
    for k in range(levels):
        input_copy(k, 0, tokens).wait_send()
        partial_copy(k, 0, tokens).wait_send()


def settle_kernel(pre, gh_sum, acc, hid, guu, gvd, gvu, gud, out, gx, gwu, gwd, guu_out, gvu_out, gud_out, gvd_out, sems):
    slabs, width, hidden = gwu.shape
    block = acc.shape[1]
    pairs = []
    for k in range(SLOTS):
        pairs.append((pre.at[pl.ds(k * width, width)], gwu.at[k]))
        pairs.append((gh_sum.at[pl.ds(0, hidden), pl.ds(k * width, width)], gwd.at[k]))
    for j in range(hidden // block):
        pairs.append((acc.at[pl.ds(hidden + j * width, width)], gwu.at[SLOTS, :, pl.ds(j * block, block)]))
    pairs.append((acc.at[pl.ds(0, hidden), pl.ds(0, width)], gwd.at[SLOTS]))
    pairs.append((hid.at[:, pl.ds(0, width)], out))
    pairs.append((hid.at[:, pl.ds(width, width)], gx))
    pairs.append((guu, guu_out))
    pairs.append((gvd, gvd_out))
    pairs.append((gvu, gvu_out))
    pairs.append((gud, gud_out))
    puts = [pltpu.make_async_copy(src, dst, sems.at[i]) for i, (src, dst) in enumerate(pairs)]
    for copy in puts:
        copy.start()
    for copy in puts:
        copy.wait()


def settled(got, outs):
    width, hidden = outs[2].shape[1:]
    copies = 2 * SLOTS + hidden // got[2].shape[1] + 7
    size = sum(a.size * a.dtype.itemsize for a in outs)
    hbm, vmem = pl.BlockSpec(memory_space=pl.ANY), pl.BlockSpec(memory_space=pltpu.VMEM)
    return pl.pallas_call(
        settle_kernel,
        in_specs=[vmem] * len(got),
        out_specs=[hbm] * len(outs),
        out_shape=outs,
        scratch_shapes=[pltpu.SemaphoreType.DMA((copies,))],
        compiler_params=pltpu.CompilerParams(vmem_limit_bytes=1024 * 1024),
        cost_estimate=pl.CostEstimate(flops=0, bytes_accessed=size, transcendentals=0),
        name="settle",
    )(*got)


def summed_over_dp(array):
    if lax.axis_size("dp") == 1:
        return array
    return lax.psum(array.astype(jnp.bfloat16), "dp").astype(jnp.float32)


def per_device(activations, w_up, w_down, u_up, v_up, u_down, v_down, mask_up, mask_down, grad_y):
    bf, f32 = jnp.bfloat16, jnp.float32
    slabs, width, hidden = w_up.shape
    tokens = activations.shape[0]
    rank = v_up.shape[0]
    levels = slabs - 1
    rounds = lax.axis_size("mp").bit_length() - 1
    vmem = pltpu.VMEM
    dma = lambda *shape: pltpu.SemaphoreType.DMA(shape)
    shape = jax.ShapeDtypeStruct
    outs = [
        shape((tokens, width), bf), shape((tokens, width), bf), shape((slabs, width, hidden), f32), shape((slabs, hidden, width), f32),
        shape((width, rank), f32), shape((rank, hidden), f32), shape((hidden, rank), f32), shape((rank, width), f32),
    ]
    scratch = [
        vmem((slabs, tokens, 2 * width), bf), vmem(w_up.shape, bf), vmem(w_down.shape, bf),
        vmem(u_up.shape, bf), vmem(v_up.shape, bf), vmem(u_down.shape, bf), vmem(v_down.shape, bf),
        vmem((tokens, hidden), bf),
        vmem((levels, tokens, 2 * width), bf), vmem((levels, tokens, 2 * width), bf), vmem((tokens, 2 * width), f32),
        vmem((tokens, 2 * rank), bf), vmem((tokens, 2 * rank), bf),
        vmem((tokens, 2 * rank), bf), vmem((tokens + (tokens >> rounds - 1), 2 * rank), bf),
        vmem((8 * levels, 128), f32), vmem((8 * levels, 128), f32),
        dma(8), dma(levels), dma(levels), dma(levels), dma(levels, CHUNKS), dma(levels), dma(levels, CHUNKS),
        dma(PARTS, 2 * rounds - 1), dma(PARTS, 2 * rounds - 1), dma(PARTS, 2 * rounds - 1), dma(PARTS, 2 * rounds - 1),
    ]
    left = [
        ((AHEAD * tokens // CHUNKS, hidden), f32), ((AHEAD * tokens // CHUNKS, hidden), f32), ((tokens, 2 * rank), f32),
        ((tokens, hidden), bf), ((width, rank), f32), ((rank, width), f32), ((rank, hidden), f32), ((hidden, rank), f32),
    ]
    taken = sum(math.prod(dims) * jnp.dtype(dtype).itemsize for dims, dtype in left)
    smem = pl.BlockSpec(memory_space=pltpu.SMEM)
    hbm = pl.BlockSpec(memory_space=pl.ANY)
    got = pl.pallas_call(
        functools.partial(kernel, rounds),
        in_specs=[smem, smem] + [hbm] * 8,
        out_specs=[pl.BlockSpec(memory_space=vmem)] * len(left),
        out_shape=[vmem(*spec) for spec in left],
        scratch_shapes=scratch,
        compiler_params=pltpu.CompilerParams(vmem_limit_bytes=VMEM_LIMIT - taken, collective_id=0, has_side_effects=True),
        name="sublayer",
    )(mask_up[:, 0], mask_down[:, 0], activations, grad_y, w_up, w_down, u_up, v_up, u_down, v_down)
    got = settled(got, outs)
    return tuple(got[:2]) + tuple(summed_over_dp(g) for g in got[2:])


def solution(mesh):
    acts, rows, columns = P("dp", "mp"), P("mp", None), P(None, "mp")
    up, down = P(None, None, "mp"), P(None, "mp", None)
    return jax.shard_map(
        per_device,
        mesh=mesh,
        in_specs=(acts, up, down, rows, columns, rows, columns, columns, columns, acts),
        out_specs=(acts, acts, up, down, rows, columns, rows, columns),
        check_vma=False,
    )
```

```python
import functools
import math

import jax
import jax.numpy as jnp
from jax import lax
from jax.experimental import pallas as pl
from jax.experimental.pallas import tpu as pltpu
from jax.sharding import PartitionSpec as P

CHUNKS = 4
PIECES = 4
PARTS = 2
AHEAD = 2
AHEAD_AT = (6, 8)
SLOTS = 4
FIRST_SLAB = 1
ROWS = 256
COLUMNS = 256
ROOT = 0.7978845608028654
CUBIC = 0.044715
VMEM_LIMIT = 67043328
MESH = pl.DeviceIdType.MESH
EARLY_ORDERS = ((0, 1, 2, 3), (0, 2, 3, 1))
LATE_ORDERS = ((0, 2, 3, 1), (0, 1, 2, 3))
EARLY_ISSUE = ((2, 2, 2), (1, 1, 1), (1, 2, 1), (1, 1, 1), (1, 1, 1), (1, 1, 1), (1, 1, 1), (1, 1, 1), (2, 2, 2))
CHUNK_ISSUE = ((2, 2, 2), (2, 2, 2), (0, 1, 2), (0, 0, 0))
LATE_ISSUE = ((2, 1, 1), (1, 1, 1), (1, 1, 1), (1, 2, 1), (2, 1, 2), (1, 1, 1), (1, 1, 1), (2, 2, 2), (4, 4, 4))


def dot(left, right):
    return jnp.dot(left, right, preferred_element_type=jnp.float32)


def dot_nt(left, right):
    return lax.dot_general(left, right, (((1,), (1,)), ((), ())), preferred_element_type=jnp.float32)


def dot_tn(left, right):
    return lax.dot_general(left, right, (((0,), (0,)), ((), ())), preferred_element_type=jnp.float32)


class Sum:
    def __init__(self, me, part, order, acc, sent, got, held, send_sems, recv_sems, apart):
        self.me, self.part, self.order = me, part, order
        self.acc, self.sent, self.got, self.held = acc, sent, got, held
        self.send_sems, self.recv_sems = send_sems, recv_sems
        self.length = acc.shape[0] // PARTS
        self.base, self.offset = jnp.int32(part * self.length), part * self.length
        self.rounds = len(order)
        self.steps = 2 * self.rounds - 1
        self.landing = acc.shape[0] + part * (self.length >> self.rounds - 1) if apart else None
        self.copy = None

    def bit(self, level):
        return lax.rem(lax.div(self.me, jnp.int32(1 << level)), jnp.int32(2))

    def rows(self, base, length):
        return pl.ds(pl.multiple_of(base, length), length)

    def remote(self, src, dst, step, level):
        self.copy = pltpu.make_async_remote_copy(
            src_ref=src, dst_ref=dst, send_sem=self.send_sems.at[self.part, step], recv_sem=self.recv_sems.at[self.part, step],
            device_id={"mp": partner(self.me, level)}, device_id_type=MESH,
        )
        self.copy.start()

    def landed(self, step, size):
        last = step == self.rounds - 1 and self.landing is not None
        return pl.ds(self.landing if last else self.offset, size)

    def start(self, step):
        if step < self.rounds:
            level = self.order[step]
            last = step == self.rounds - 1
            size = self.length if last else self.length // 2
            base = self.base if last else self.base + (1 - self.bit(level)) * size
            here = pl.ds(self.offset, size)
            self.sent[here, :] = self.acc[self.rows(base, size), :].astype(jnp.bfloat16)
            self.remote(self.sent.at[here], self.got.at[self.landed(step, size)], step, level)
        else:
            mine = self.held.at[self.rows(self.base, self.length)]
            self.remote(mine, mine, step, self.order[self.steps - 1 - step])

    def finish(self, step):
        self.copy.wait()
        if step < self.rounds:
            last = step == self.rounds - 1
            size = self.length if last else self.length // 2
            if not last:
                self.base = self.base + self.bit(self.order[step]) * size
            kept = self.rows(self.base, size)
            total = self.acc[kept, :] + self.got[self.landed(step, size), :].astype(jnp.float32)
            if last:
                self.held[kept, :] = total.astype(jnp.bfloat16)
            else:
                self.acc[kept, :] = total
            self.offset += size
            self.length = size
        else:
            self.base = self.base - self.bit(self.order[self.steps - 1 - step]) * self.length
            self.length *= 2

    def advance(self, step):
        if step > 0:
            self.finish(step - 1)
        if step < self.steps:
            self.start(step)


def partner(me, level):
    step = 1 << level
    bit = lax.rem(lax.div(me, jnp.int32(step)), jnp.int32(2))
    return me + (1 - 2 * bit) * step


def kernel(rounds, mu_ref, md_ref, x_hbm, gy_hbm, wu_hbm, wd_hbm, uu_hbm, vu_hbm, ud_hbm, vd_hbm,
           pre, gh_sum, acc, hid, guu, gvd, gvu, gud,
           xs, wu, wd, uu, vu, ud, vd, gp, put, came, diag, zs, zl, sent, got, mask_mine, mask_theirs,
           load_sems, mask_send, mask_recv, in_send, in_recv, put_send, put_recv, es, er, ls, lr):
    slabs, tokens = xs.shape[:2]
    levels = slabs - 1
    width, hidden = wu.shape[1:]
    rank = vu.shape[0]
    chunk = tokens // CHUNKS
    piece = chunk // PIECES
    pieces = CHUNKS * PIECES
    step = min(COLUMNS, hidden)
    me = lax.axis_index("mp")

    loads = []
    for i, (src, dst) in enumerate((
        (x_hbm, xs.at[0, :, pl.ds(0, width)]), (gy_hbm, xs.at[0, :, pl.ds(width, width)]),
        (uu_hbm, uu), (vd_hbm, vd), (wu_hbm, wu), (wd_hbm, wd), (vu_hbm, vu), (ud_hbm, ud),
    )):
        loads.append(pltpu.make_async_copy(src, dst, load_sems.at[i]))
        loads[-1].start()

    barrier = pltpu.get_barrier_semaphore()
    for level in range(rounds):
        pl.semaphore_signal(barrier, inc=1, device_id={"mp": partner(me, level)}, device_id_type=MESH)
    for k in range(levels):
        mask_mine[8 * k:8 * k + 8, :] = jnp.full((8, 128), md_ref[k].astype(jnp.float32))
    pl.semaphore_wait(barrier, rounds)

    def mask_copy(k):
        here = pl.ds(8 * k, 8)
        return pltpu.make_async_remote_copy(
            src_ref=mask_mine.at[here], dst_ref=mask_theirs.at[here], send_sem=mask_send.at[k], recv_sem=mask_recv.at[k],
            device_id={"mp": partner(me, k)}, device_id_type=MESH)

    def input_copy(k, start, length):
        rows = pl.ds(start, length)
        return pltpu.make_async_remote_copy(
            src_ref=xs.at[0, rows], dst_ref=xs.at[k + 1, rows], send_sem=in_send.at[k], recv_sem=in_recv.at[k, lax.div(start, chunk)],
            device_id={"mp": partner(me, k)}, device_id_type=MESH)

    def partial_copy(k, start, length):
        rows = pl.ds(start, length)
        return pltpu.make_async_remote_copy(
            src_ref=put.at[k, rows], dst_ref=came.at[k, rows], send_sem=put_send.at[k], recv_sem=put_recv.at[k, lax.div(start, chunk)],
            device_id={"mp": partner(me, k)}, device_id_type=MESH)

    in_done = [0] * levels
    put_done = [0] * levels

    def issue(copy, done, k, count):
        for i in range(done[k], min(pieces, done[k] + count)):
            copy(k, i * piece, piece).start()
        done[k] = min(pieces, done[k] + count)

    loads[0].wait()
    loads[1].wait()
    for k in range(levels):
        mask_copy(k).start()
    issue(input_copy, in_done, 0, PIECES)
    for k in range(1, levels):
        issue(input_copy, in_done, k, EARLY_ISSUE[0][k - 1])
    loads[2].wait()
    loads[3].wait()

    @pl.loop(0, CHUNKS)
    def _(c):
        rows = pl.ds(pl.multiple_of(c * chunk, chunk), chunk)
        acc[rows, :rank] = dot(xs[0, rows, :width], uu[...])
        acc[rows, rank:] = dot_nt(xs[0, rows, width:], vd[...])

    def sums(rows, start):
        cols = slice(start, start + step)
        v = dot(xs[0, rows, :width], wu[0, :, cols])
        gh = dot_nt(xs[0, rows, width:], wd[0, cols, :])
        for k in range(1, slabs):
            v += dot(xs[k, rows, :width], wu[k, :, cols])
            gh += dot_nt(xs[k, rows, width:], wd[k, cols, :])
        return v, gh

    def sums_ahead(c):
        for k in range(levels):
            input_copy(k, c * chunk, chunk).wait_recv()

        @pl.loop(0, chunk // ROWS)
        def _(r):
            rows = pl.ds(pl.multiple_of(c * chunk + r * ROWS, ROWS), ROWS)
            for start in range(0, hidden, step):
                pre[rows, start:start + step], gh_sum[rows, start:start + step] = sums(rows, start)

    tail = tuple(range(levels, rounds))
    early = [
        Sum(me, 0, EARLY_ORDERS[0] + tail, acc, sent, got, zs, es, er, False),
        Sum(me, 1, EARLY_ORDERS[1] + tail, acc, sent, got, zs, es, er, False),
    ]
    for s in range(2 * rounds):
        for part in early:
            part.advance(s)
        if s == 0:
            issue(input_copy, in_done, 0, pieces)
        elif s < len(EARLY_ISSUE):
            for k in range(1, levels):
                issue(input_copy, in_done, k, EARLY_ISSUE[s][k - 1])
        if s == 0:
            loads[4].wait()
            for k in range(levels):
                wu[k + 1] = (wu[k + 1].astype(jnp.float32) * mu_ref[k].astype(jnp.float32)).astype(jnp.bfloat16)
        if s == 1:
            loads[5].wait()
            for k in range(levels):
                mask_copy(k).wait()
                row = jnp.concatenate([mask_theirs[8 * k:8 * k + 1, :]] * (width // 128), axis=1)
                wd[k + 1] = (wd[k + 1].astype(jnp.float32) * row).astype(jnp.bfloat16)
        if s == 2:
            loads[6].wait()
            loads[7].wait()
        if s in AHEAD_AT:
            sums_ahead(AHEAD_AT.index(s))
    for k in range(1, levels):
        issue(input_copy, in_done, k, pieces)

    def products(c, chunks, ahead):
        @pl.loop(0, chunk // ROWS)
        def _(r):
            rows = pl.ds(pl.multiple_of(c * chunk + r * ROWS, ROWS), ROWS)
            for start in range(0, hidden, step):
                cols = slice(start, start + step)
                v, gh = (pre[rows, cols], gh_sum[rows, cols]) if ahead else sums(rows, start)
                v += dot(zs[rows, :rank], vu[:, cols])
                gh += dot_nt(zs[rows, rank:], ud[cols, :])
                square = v * v
                half_tanh = 0.5 * jnp.tanh(v * (ROOT + (ROOT * CUBIC) * square))
                gate = 0.5 + half_tanh
                hid[rows, cols] = (v * gate).astype(jnp.bfloat16)
                slope = gate + v * (0.5 - 2.0 * half_tanh * half_tanh) * (ROOT + (3.0 * ROOT * CUBIC) * square)
                gp[rows, cols] = (gh * slope).astype(jnp.bfloat16)
            h = hid[rows, :]
            g = gp[rows, :]
            for k in range(levels):
                put[k, rows, :width] = dot(h, wd[k + 1]).astype(jnp.bfloat16)
                put[k, rows, width:] = dot_nt(g, wu[k + 1]).astype(jnp.bfloat16)
            acc[rows, :rank] = dot(h, ud[...])
            acc[rows, rank:] = dot_nt(g, vu[...])
            diag[rows, :width] = dot(h, wd[0])
            diag[rows, width:] = dot_nt(g, wu[0])

        partial_copy(0, c * chunk, chunk).start()
        for k in range(1, levels):
            for at in chunks:
                first = sum(row[k - 1] for row in CHUNK_ISSUE[:at])

                @pl.when(c == at)
                def _():
                    for i in range(first, first + CHUNK_ISSUE[at][k - 1]):
                        partial_copy(k, i * piece, piece).start()

    @pl.loop(0, AHEAD)
    def _(c):
        products(c, range(AHEAD), True)

    @pl.loop(AHEAD, CHUNKS)
    def _(c):
        for k in range(levels):
            input_copy(k, c * chunk, chunk).wait_recv()
        products(c, range(AHEAD, CHUNKS), False)

    for k in range(levels):
        put_done[k] = pieces if k == 0 else sum(row[k - 1] for row in CHUNK_ISSUE)

    def slab_grads(k):
        for start in range(0, width, ROWS):
            stop = min(width, start + ROWS)
            up = dot_tn(xs[k, :, start:stop], gp[...])
            if k:
                up = up * mu_ref[k - 1].astype(jnp.float32)
            if k < SLOTS:
                pre[k * width + start:k * width + stop, :] = up
            else:
                for j in range(hidden // (2 * rank)):
                    base = hidden + j * width
                    acc[base + start:base + stop, :] = up[:, j * 2 * rank:(j + 1) * 2 * rank]

        @pl.loop(0, hidden // step)
        def _(b):
            cols = pl.ds(pl.multiple_of(b * step, step), step)
            down = dot_tn(hid[:, cols], xs[k, :, width:])
            if k:
                down = down * jnp.concatenate([mask_theirs[8 * k - 8:8 * k - 7, :]] * (width // 128), axis=1)
            if k < SLOTS:
                gh_sum[cols, k * width:(k + 1) * width] = down
            else:
                acc[cols, :width] = down

    def rank_grads():
        gvu[...] = dot_tn(zs[:, :rank], gp[...])
        gud[...] = dot_tn(hid[...], zs[:, rank:])

    late = [
        Sum(me, 0, LATE_ORDERS[0] + tail, acc, sent, got, zl, ls, lr, True),
        Sum(me, 1, LATE_ORDERS[1] + tail, acc, sent, got, zl, ls, lr, True),
    ]
    for s in range(2 * rounds):
        for part in late:
            part.advance(s)
        if s < len(LATE_ISSUE):
            for k in range(1, levels):
                issue(partial_copy, put_done, k, LATE_ISSUE[s][k - 1])
        if FIRST_SLAB <= s < FIRST_SLAB + SLOTS:
            slab_grads(s - FIRST_SLAB)
        if s == rounds + 2:
            rank_grads()
        if s == rounds + 1:
            slab_grads(SLOTS)
    for k in range(1, levels):
        issue(partial_copy, put_done, k, pieces)

    guu[...] = dot_tn(xs[0, :, :width], zl[:, rank:])
    gvd[...] = dot_tn(zl[:, :rank], xs[0, :, width:])

    for c in range(CHUNKS):
        rows = pl.ds(c * chunk, chunk)
        out = diag[rows, :width] + dot(zl[rows, :rank], vd[...])
        gx = diag[rows, width:] + dot_nt(zl[rows, rank:], uu[...])
        for k in range(levels):
            partial_copy(k, c * chunk, chunk).wait_recv()
            out = out + came[k, rows, :width].astype(jnp.float32)
            gx = gx + came[k, rows, width:].astype(jnp.float32)
        hid[rows, :width] = out.astype(jnp.bfloat16)
        hid[rows, width:2 * width] = gx.astype(jnp.bfloat16)
    for k in range(levels):
        input_copy(k, 0, tokens).wait_send()
        partial_copy(k, 0, tokens).wait_send()


def settle_kernel(pre, gh_sum, acc, hid, guu, gvd, gvu, gud, out, gx, gwu, gwd, guu_out, gvu_out, gud_out, gvd_out, sems):
    slabs, width, hidden = gwu.shape
    block = acc.shape[1]
    pairs = []
    for k in range(SLOTS):
        pairs.append((pre.at[pl.ds(k * width, width)], gwu.at[k]))
        pairs.append((gh_sum.at[pl.ds(0, hidden), pl.ds(k * width, width)], gwd.at[k]))
    for j in range(hidden // block):
        pairs.append((acc.at[pl.ds(hidden + j * width, width)], gwu.at[SLOTS, :, pl.ds(j * block, block)]))
    pairs.append((acc.at[pl.ds(0, hidden), pl.ds(0, width)], gwd.at[SLOTS]))
    pairs.append((hid.at[:, pl.ds(0, width)], out))
    pairs.append((hid.at[:, pl.ds(width, width)], gx))
    pairs.append((guu, guu_out))
    pairs.append((gvd, gvd_out))
    pairs.append((gvu, gvu_out))
    pairs.append((gud, gud_out))
    puts = [pltpu.make_async_copy(src, dst, sems.at[i]) for i, (src, dst) in enumerate(pairs)]
    for copy in puts:
        copy.start()
    for copy in puts:
        copy.wait()


def settled(got, outs):
    width, hidden = outs[2].shape[1:]
    copies = 2 * SLOTS + hidden // got[2].shape[1] + 7
    size = sum(a.size * a.dtype.itemsize for a in outs)
    hbm, vmem = pl.BlockSpec(memory_space=pl.ANY), pl.BlockSpec(memory_space=pltpu.VMEM)
    return pl.pallas_call(
        settle_kernel,
        in_specs=[vmem] * len(got),
        out_specs=[hbm] * len(outs),
        out_shape=outs,
        scratch_shapes=[pltpu.SemaphoreType.DMA((copies,))],
        compiler_params=pltpu.CompilerParams(vmem_limit_bytes=1024 * 1024),
        cost_estimate=pl.CostEstimate(flops=0, bytes_accessed=size, transcendentals=0),
        name="settle",
    )(*got)


def summed_over_dp(array):
    if lax.axis_size("dp") == 1:
        return array
    return lax.psum(array.astype(jnp.bfloat16), "dp").astype(jnp.float32)


def per_device(activations, w_up, w_down, u_up, v_up, u_down, v_down, mask_up, mask_down, grad_y):
    bf, f32 = jnp.bfloat16, jnp.float32
    slabs, width, hidden = w_up.shape
    tokens = activations.shape[0]
    rank = v_up.shape[0]
    levels = slabs - 1
    rounds = lax.axis_size("mp").bit_length() - 1
    vmem = pltpu.VMEM
    dma = lambda *shape: pltpu.SemaphoreType.DMA(shape)
    shape = jax.ShapeDtypeStruct
    outs = [
        shape((tokens, width), bf), shape((tokens, width), bf), shape((slabs, width, hidden), f32), shape((slabs, hidden, width), f32),
        shape((width, rank), f32), shape((rank, hidden), f32), shape((hidden, rank), f32), shape((rank, width), f32),
    ]
    scratch = [
        vmem((slabs, tokens, 2 * width), bf), vmem(w_up.shape, bf), vmem(w_down.shape, bf),
        vmem(u_up.shape, bf), vmem(v_up.shape, bf), vmem(u_down.shape, bf), vmem(v_down.shape, bf),
        vmem((tokens, hidden), bf),
        vmem((levels, tokens, 2 * width), bf), vmem((levels, tokens, 2 * width), bf), vmem((tokens, 2 * width), f32),
        vmem((tokens, 2 * rank), bf), vmem((tokens, 2 * rank), bf),
        vmem((tokens, 2 * rank), bf), vmem((tokens + (tokens >> rounds - 1), 2 * rank), bf),
        vmem((8 * levels, 128), f32), vmem((8 * levels, 128), f32),
        dma(8), dma(levels), dma(levels), dma(levels), dma(levels, CHUNKS), dma(levels), dma(levels, CHUNKS),
        dma(PARTS, 2 * rounds - 1), dma(PARTS, 2 * rounds - 1), dma(PARTS, 2 * rounds - 1), dma(PARTS, 2 * rounds - 1),
    ]
    left = [
        ((AHEAD * tokens // CHUNKS, hidden), f32), ((AHEAD * tokens // CHUNKS, hidden), f32), ((tokens, 2 * rank), f32),
        ((tokens, hidden), bf), ((width, rank), f32), ((rank, width), f32), ((rank, hidden), f32), ((hidden, rank), f32),
    ]
    taken = sum(math.prod(dims) * jnp.dtype(dtype).itemsize for dims, dtype in left)
    smem = pl.BlockSpec(memory_space=pltpu.SMEM)
    hbm = pl.BlockSpec(memory_space=pl.ANY)
    got = pl.pallas_call(
        functools.partial(kernel, rounds),
        in_specs=[smem, smem] + [hbm] * 8,
        out_specs=[pl.BlockSpec(memory_space=vmem)] * len(left),
        out_shape=[vmem(*spec) for spec in left],
        scratch_shapes=scratch,
        compiler_params=pltpu.CompilerParams(vmem_limit_bytes=VMEM_LIMIT - taken, collective_id=0, has_side_effects=True),
        name="sublayer",
    )(mask_up[:, 0], mask_down[:, 0], activations, grad_y, w_up, w_down, u_up, v_up, u_down, v_down)
    got = settled(got, outs)
    return tuple(got[:2]) + tuple(summed_over_dp(g) for g in got[2:])


def solution(mesh):
    acts, rows, columns = P("dp", "mp"), P("mp", None), P(None, "mp")
    up, down = P(None, None, "mp"), P(None, "mp", None)
    return jax.shard_map(
        per_device,
        mesh=mesh,
        in_specs=(acts, up, down, rows, columns, rows, columns, columns, columns, acts),
        out_specs=(acts, acts, up, down, rows, columns, rows, columns),
        check_vma=False,
    )
```
